32 devices in a mesh: seq: 4 (over y, x), shard: 8 (over z, core).
Axes of the slice: x: 2, y: 2, z: 4, core: 2. Of those that a mesh axis runs over, the one named last changes fastest.
Arguments:
- layer_input: bfloat16 [8, 2048, 1024], P('shard', 'seq'), may hold values from -6 to 6
- cotangent: float32 [8, 2048, 1024], P('shard', 'seq'), may hold values from -6 to 6
- weight_qkv: float32 [1024, 3072], P(('seq', 'shard')), may hold values from -0.3125 to 0.3125
- weight_merge: float32 [1024, 1024], P(('seq', 'shard')), may hold values from -0.3125 to 0.3125
- weight_expand: float32 [1024, 4096], P(('seq', 'shard')), may hold values from -0.1875 to 0.1875
- weight_shrink: float32 [4096, 1024], P(('seq', 'shard')), may hold values from -0.09375 to 0.09375
- norm_gains: float32 [2, 1024], P(None, ('seq', 'shard')), may hold values from 0.5 to 1.5
- all_biases: float32 [6, 1024], P(None, ('seq', 'shard')), may hold values from -2 to 2
- bias_hidden: float32 [4096], P(('seq', 'shard')), may hold values from -2 to 2
- moment_qkv: float32 [1024, 3072], P(('seq', 'shard')), may hold values from -96 to 96
- moment_merge: float32 [1024, 1024], P(('seq', 'shard')), may hold values from -96 to 96
- moment_expand: float32 [1024, 4096], P(('seq', 'shard')), may hold values from -96 to 96
- moment_shrink: float32 [4096, 1024], P(('seq', 'shard')), may hold values from -96 to 96
- moment_gains: float32 [2, 1024], P(None, ('seq', 'shard')), may hold values from -96 to 96
- moment_biases: float32 [6, 1024], P(None, ('seq', 'shard')), may hold values from -96 to 96
- moment_hidden: float32 [4096], P(('seq', 'shard')), may hold values from -96 to 96
- squares_qkv: float32 [1024, 3072], P(('seq', 'shard')), may hold values from 4.096 to 40.96
- squares_merge: float32 [1024, 1024], P(('seq', 'shard')), may hold values from 4.096 to 40.96
- squares_expand: float32 [1024, 4096], P(('seq', 'shard')), may hold values from 4.096 to 40.96
- squares_shrink: float32 [4096, 1024], P(('seq', 'shard')), may hold values from 4.096 to 40.96
- squares_gains: float32 [2, 1024], P(None, ('seq', 'shard')), may hold values from 4.096 to 40.96
- squares_biases: float32 [6, 1024], P(None, ('seq', 'shard')), may hold values from 4.096 to 40.96
- squares_hidden: float32 [4096], P(('seq', 'shard')), may hold values from 4.096 to 40.96
Outputs:
- layer_output: bfloat16 [8, 2048, 1024], P('shard', 'seq')
- grad_input: float32 [8, 2048, 1024], P('shard', 'seq')
- grad_qkv: float32 [1024, 3072], P(('seq', 'shard'))
- grad_merge: float32 [1024, 1024], P(('seq', 'shard'))
- grad_expand: float32 [1024, 4096], P(('seq', 'shard'))
- grad_shrink: float32 [4096, 1024], P(('seq', 'shard'))
- grad_gains: float32 [2, 1024], P(None, ('seq', 'shard'))
- grad_biases: float32 [6, 1024], P(None, ('seq', 'shard'))
- grad_hidden: float32 [4096], P(('seq', 'shard'))
- master_qkv: float32 [1024, 3072], P(('seq', 'shard'))
- master_merge: float32 [1024, 1024], P(('seq', 'shard'))
- master_expand: float32 [1024, 4096], P(('seq', 'shard'))
- master_shrink: float32 [4096, 1024], P(('seq', 'shard'))
- change_gains: float32 [2, 1024], P(None, ('seq', 'shard'))
- change_biases: float32 [6, 1024], P(None, ('seq', 'shard'))
- change_hidden: float32 [4096], P(('seq', 'shard'))
- momentum_qkv: float32 [1024, 3072], P(('seq', 'shard'))
- momentum_merge: float32 [1024, 1024], P(('seq', 'shard'))
- momentum_expand: float32 [1024, 4096], P(('seq', 'shard'))
- momentum_shrink: float32 [4096, 1024], P(('seq', 'shard'))
- momentum_gains: float32 [2, 1024], P(None, ('seq', 'shard'))
- momentum_biases: float32 [6, 1024], P(None, ('seq', 'shard'))
- momentum_hidden: float32 [4096], P(('seq', 'shard'))
- squared_qkv: float32 [1024, 3072], P(('seq', 'shard'))
- squared_merge: float32 [1024, 1024], P(('seq', 'shard'))
- squared_expand: float32 [1024, 4096], P(('seq', 'shard'))
- squared_shrink: float32 [4096, 1024], P(('seq', 'shard'))
- squared_gains: float32 [2, 1024], P(None, ('seq', 'shard'))
- squared_biases: float32 [6, 1024], P(None, ('seq', 'shard'))
- squared_hidden: float32 [4096], P(('seq', 'shard'))
The draws below stay inside these ranges and needn't reach their ends.
All inputs are finite; a program needn't handle non-finite values.
Results may differ from the reference program's by a relative error of at most 0.014.
The reference program's roundings to bfloat16 on the way count: a program that leaves them out, or rounds other values in their place, can miss the bound.
Values may be sent and summed in bfloat16 or wider, within the bound.
No kernel may reach another device: no remote copies, remote signals or barrier semaphores. Data moves between devices by JAX's collectives and lax.ppermute only.
A program may use at most 192 MiB of HBM per device.

```python
import math
import jax
import jax.numpy as jnp
from jax import lax

D = 1024
H = 16
HD = 64
FF = 4096
STEP = 10
LEN = 2048
SEQS = 8
TOKENS = 16384


def block_scale(key, shape, cuts, low, largest):
    loudness, own = 1.0, jax.random.fold_in(key, 6)
    for dim, parts in cuts:
        steps = jnp.exp(jax.random.uniform(jax.random.fold_in(own, dim), (parts,), jnp.float32, low / len(cuts), largest / len(cuts)))
        loudness = loudness * jnp.repeat(steps, shape[dim] // parts).reshape([-1 if axis == dim else 1 for axis in range(len(shape))])
    return loudness


def noise(own_key, shape, scale, limit, shards=(), kind=jnp.bfloat16):
    array = jax.random.normal(own_key, shape, jnp.float32) * scale
    if len(shards) > 0:
        array = block_scale(own_key, shape, shards, -0.22, 0.18) * array
    return jnp.clip(array, min=-limit, max=limit).astype(kind)


def setup_inputs(seed: int = 0) -> dict:
    key_of = jax.random.split(jax.random.key(seed), 24)
    layer_input = noise(key_of[0], (SEQS, LEN, D), 1.0, 6.0, ((0, 8), (1, 4)))
    cotangent = noise(key_of[1], (SEQS, LEN, D), 1.0, 6.0, ((0, 8), (1, 4)), jnp.float32)
    weight_qkv = noise(key_of[2], (D, 3 * D), (D * 2 // 5) ** -0.5, 0.3125, ((0, 32),), jnp.float32)
    weight_merge = noise(key_of[3], (D, D), (D * 5 // 16) ** -0.5, 0.3125, ((0, 32),), jnp.float32)
    weight_expand = noise(key_of[4], (D, FF), D ** -0.5, 0.1875, ((0, 32),), jnp.float32)
    weight_shrink = noise(key_of[5], (FF, D), FF ** -0.5, 0.09375, ((0, 32),), jnp.float32)
    norm_gains = jnp.clip(1.0 + 0.1 * jax.random.normal(key_of[6], (2, D), jnp.float32), 0.5, 1.5)
    all_biases = noise(key_of[7], (6, D), 0.15, 2.0, ((1, 32),), jnp.float32)
    bias_hidden = noise(key_of[8], (FF,), 0.15, 2.0, ((0, 32),), jnp.float32)
    moment_qkv = noise(key_of[9], (D, 3 * D), (TOKENS ** 0.5 / 8), 96.0, ((0, 32),), jnp.float32)
    moment_merge = noise(key_of[10], (D, D), (TOKENS ** 0.5 / 8), 96.0, ((0, 32),), jnp.float32)
    moment_expand = noise(key_of[11], (D, FF), (TOKENS ** 0.5 / 8), 96.0, ((0, 32),), jnp.float32)
    moment_shrink = noise(key_of[12], (FF, D), (TOKENS ** 0.5 / 8), 96.0, ((0, 32),), jnp.float32)
    moment_gains = noise(key_of[13], (2, D), (TOKENS ** 0.5 / 8), 96.0, ((1, 32),), jnp.float32)
    moment_biases = noise(key_of[14], (6, D), (TOKENS ** 0.5 / 8), 96.0, ((1, 32),), jnp.float32)
    moment_hidden = noise(key_of[15], (FF,), (TOKENS ** 0.5 / 8), 96.0, ((0, 32),), jnp.float32)
    squares_qkv = jnp.clip(jnp.exp(math.log(40.96) - 2.30258502 * jax.random.uniform(key_of[16], (D, 3 * D), jnp.float32) ** block_scale(key_of[16], (D, 3 * D), ((0, 32),), -0.2, 0.2)), 4.096, 40.96)
    squares_merge = jnp.clip(jnp.exp(math.log(40.96) - 2.30258502 * jax.random.uniform(key_of[17], (D, D), jnp.float32) ** block_scale(key_of[17], (D, D), ((0, 32),), -0.2, 0.2)), 4.096, 40.96)
    squares_expand = jnp.clip(jnp.exp(math.log(40.96) - 2.30258502 * jax.random.uniform(key_of[18], (D, FF), jnp.float32) ** block_scale(key_of[18], (D, FF), ((0, 32),), -0.2, 0.2)), 4.096, 40.96)
    squares_shrink = jnp.clip(jnp.exp(math.log(40.96) - 2.30258502 * jax.random.uniform(key_of[19], (FF, D), jnp.float32) ** block_scale(key_of[19], (FF, D), ((0, 32),), -0.2, 0.2)), 4.096, 40.96)
    squares_gains = jnp.clip(jnp.exp(math.log(40.96) - 2.30258502 * jax.random.uniform(key_of[20], (2, D), jnp.float32) ** block_scale(key_of[20], (2, D), ((1, 32),), -0.2, 0.2)), 4.096, 40.96)
    squares_biases = jnp.clip(jnp.exp(math.log(40.96) - 2.30258502 * jax.random.uniform(key_of[21], (6, D), jnp.float32) ** block_scale(key_of[21], (6, D), ((1, 32),), -0.2, 0.2)), 4.096, 40.96)
    squares_hidden = jnp.clip(jnp.exp(math.log(40.96) - 2.30258502 * jax.random.uniform(key_of[22], (FF,), jnp.float32) ** block_scale(key_of[22], (FF,), ((0, 32),), -0.2, 0.2)), 4.096, 40.96)
    return {"layer_input": layer_input, "cotangent": cotangent, "weight_qkv": weight_qkv, "weight_merge": weight_merge, "weight_expand": weight_expand, "weight_shrink": weight_shrink, "norm_gains": norm_gains, "all_biases": all_biases, "bias_hidden": bias_hidden, "moment_qkv": moment_qkv, "moment_merge": moment_merge, "moment_expand": moment_expand, "moment_shrink": moment_shrink, "moment_gains": moment_gains, "moment_biases": moment_biases, "moment_hidden": moment_hidden, "squares_qkv": squares_qkv, "squares_merge": squares_merge, "squares_expand": squares_expand, "squares_shrink": squares_shrink, "squares_gains": squares_gains, "squares_biases": squares_biases, "squares_hidden": squares_hidden}


@jax.custom_vjp
def low(v):
    return lax.optimization_barrier(v.astype(jnp.bfloat16)).astype(jnp.float32)

@jax.custom_vjp
def low_back(v):
    return v

def low_keep(v):
    return (low(v), None)

def low_pass(kept, grad):
    return (grad,)

def back_keep(v):
    return (v, None)

def back_low(kept, grad):
    return (low(grad),)
low.defvjp(low_keep, low_pass)
low_back.defvjp(back_keep, back_low)

def matmul(left, right):
    return jnp.dot(left, right, precision=lax.Precision.HIGHEST, preferred_element_type=jnp.float32)

def layer_norm(value, gain, shift):
    centre = value - lax.optimization_barrier(jnp.mean(value, axis=-1, keepdims=True))
    spread = lax.optimization_barrier(jnp.mean(centre * centre, axis=-1, keepdims=True))
    return centre * lax.rsqrt(spread + 1e-06) * gain + shift

def attend_block(piece, keys, values):
    raw = jnp.einsum('qhd,khd->hqk', piece, keys, precision=lax.Precision.HIGHEST) * 0.125
    scores = low_back(raw)
    totals = jax.nn.logsumexp(scores, axis=-1, keepdims=True)
    probs = low(jnp.exp(scores - totals))
    return jnp.einsum('hqk,khd->qhd', probs, values, precision=lax.Precision.HIGHEST)

def sequence_forward(tokens, weight_qkv, weight_merge, weight_expand, weight_shrink, norm_gains, all_biases, bias_hidden):
    length = tokens.shape[0]
    zero_row = jnp.zeros((D,), jnp.float32)
    qkv = matmul(tokens, weight_qkv) + jnp.concatenate([all_biases[1], zero_row, all_biases[2]])
    qkv = low(low_back(qkv)).reshape(length, 3, H, HD)
    query = qkv[:, 0]
    keys = qkv[:, 1]
    values = qkv[:, 2]
    block = min(512, length)
    pieces = query.reshape(length // block, block, H, HD)
    context = lax.map(jax.checkpoint(lambda piece: attend_block(piece, keys, values)), pieces)
    context = low(low_back(context.reshape(length, D)))
    attended = low_back(matmul(context, weight_merge) + all_biases[3])
    first = layer_norm(tokens + attended, norm_gains[0], all_biases[0])
    hidden = low_back(matmul(low(first), weight_expand) + bias_hidden)
    active = low(jax.nn.gelu(hidden, approximate=False))
    branch = low_back(matmul(active, weight_shrink) + all_biases[5])
    return layer_norm(first + branch, norm_gains[1], all_biases[4])

def adam_update(param, grad, moment, squares, decay):
    momentum = 0.9 * moment + 0.1 * grad
    squared = 0.999 * squares + 0.001 * grad * grad
    update = momentum / (1.0 - 0.9 ** STEP) / (jnp.sqrt(squared / (1.0 - 0.999 ** STEP)) + 1e-08)
    if decay:
        update = update + 0.01 * param
    change = -0.02 * update
    return (param - 0.02 * update, change, momentum, squared)

def reference(layer_input, cotangent, weight_qkv, weight_merge, weight_expand, weight_shrink, norm_gains, all_biases, bias_hidden, moment_qkv, moment_merge, moment_expand, moment_shrink, moment_gains, moment_biases, moment_hidden, squares_qkv, squares_merge, squares_expand, squares_shrink, squares_gains, squares_biases, squares_hidden):
    params = (weight_qkv, weight_merge, weight_expand, weight_shrink, norm_gains, all_biases, bias_hidden)
    moments = (moment_qkv, moment_merge, moment_expand, moment_shrink, moment_gains, moment_biases, moment_hidden)
    squares = (squares_qkv, squares_merge, squares_expand, squares_shrink, squares_gains, squares_biases, squares_hidden)

    def forward(tokens, *weights):
        rounded = [low(weight) for weight in weights]
        return sequence_forward(tokens, *rounded)

    def one_sequence(totals, pair):
        tokens, grad_out = pair
        result, pull = jax.vjp(forward, tokens.astype(jnp.float32), *params)
        grads = pull(grad_out)
        totals = tuple((total + grad for total, grad in zip(totals, grads[1:])))
        return (totals, (result.astype(jnp.bfloat16), grads[0]))
    zeros = tuple((jnp.zeros_like(param) for param in params))
    totals, stacked = lax.scan(one_sequence, zeros, (layer_input, cotangent))
    layer_output, grad_input = stacked
    grad_qkv, grad_merge, grad_expand, grad_shrink, grad_gains, grad_biases, grad_hidden = totals
    updated = [adam_update(params[index], totals[index], moments[index], squares[index], index < 4) for index in range(7)]
    master_qkv, unused_one, momentum_qkv, squared_qkv = updated[0]
    master_merge, unused_two, momentum_merge, squared_merge = updated[1]
    master_expand, unused_three, momentum_expand, squared_expand = updated[2]
    master_shrink, unused_four, momentum_shrink, squared_shrink = updated[3]
    unused_five, change_gains, momentum_gains, squared_gains = updated[4]
    unused_six, change_biases, momentum_biases, squared_biases = updated[5]
    unused_seven, change_hidden, momentum_hidden, squared_hidden = updated[6]
    return (layer_output, grad_input, grad_qkv, grad_merge, grad_expand, grad_shrink, grad_gains, grad_biases, grad_hidden, master_qkv, master_merge, master_expand, master_shrink, change_gains, change_biases, change_hidden, momentum_qkv, momentum_merge, momentum_expand, momentum_shrink, momentum_gains, momentum_biases, momentum_hidden, squared_qkv, squared_merge, squared_expand, squared_shrink, squared_gains, squared_biases, squared_hidden)
```

```python
import functools

import jax
import jax.numpy as jnp
from jax import lax
from jax.experimental import pallas as pl
from jax.experimental.pallas import tpu as pltpu
from jax.sharding import PartitionSpec as P

HD = 64
STEP = 10
F32 = jnp.float32
BF16 = jnp.bfloat16
NT = (((1,), (1,)), ((), ()))
NN = (((1,), (0,)), ((), ()))
TN = (((0,), (0,)), ((), ()))


def norm_forward(value, gain, shift):
    centre = value - jnp.mean(value, axis=-1, keepdims=True)
    inverse = lax.rsqrt(jnp.mean(centre * centre, axis=-1, keepdims=True) + 1e-06)
    normed = centre * inverse
    return (normed * gain + shift, normed, inverse)


def norm_backward(grad, normed, inverse, gain):
    scaled = grad * gain
    inner = jnp.mean(scaled * normed, axis=-1, keepdims=True)
    return inverse * (scaled - jnp.mean(scaled, axis=-1, keepdims=True) - normed * inner)


def gelu_slope(hidden):
    return (
        0.5 * (1.0 + lax.erf(hidden * 0.7071067811865476))
        + hidden * jnp.exp(-0.5 * hidden * hidden) * 0.3989422804014327
    )


def adam_update(param, grad, moment, squares, decay):
    momentum = 0.9 * moment + 0.1 * grad
    squared = 0.999 * squares + 0.001 * grad * grad
    update = momentum / (1.0 - 0.9**STEP) / (jnp.sqrt(squared / (1.0 - 0.999**STEP)) + 1e-08)
    if decay:
        update = update + 0.01 * param
    change = -0.02 * update
    return (param - 0.02 * update, change, momentum, squared)


def forward_kernel(q_ref, k_ref, v_ref, c_ref, total_ref, flipped_ref):
    @pl.when(pl.program_id(0) == 0)
    def _():
        flipped_ref[...] = jnp.transpose(v_ref[...])

    query = q_ref[...] * jnp.asarray(0.125, BF16)
    lane = lax.broadcasted_iota(jnp.int32, query.shape, 1)
    pieces, rows = [], []
    for head in range(2):
        own = (lane >= HD * head) & (lane < HD * head + HD)
        scores = lax.dot_general(
            k_ref[...], jnp.where(own, query, jnp.zeros_like(query)), NT, preferred_element_type=F32
        )
        highest = jnp.max(scores, axis=0, keepdims=True)
        weights = jnp.exp(scores - highest)
        total = jnp.sum(weights, axis=0, keepdims=True)
        context = lax.dot_general(
            flipped_ref[HD * head : HD * head + HD, :],
            weights.astype(BF16),
            NN,
            preferred_element_type=F32,
        )
        pieces.append(context * (1.0 / total))
        rows.append(highest + jnp.log(total))
    c_ref[...] = jnp.transpose(jnp.concatenate(pieces, axis=0)).astype(BF16)
    total_ref[...] = jnp.concatenate(rows, axis=0)[None]


def attend_forward(query, keys, values, pair, block):
    length = query.shape[0]
    whole = pl.BlockSpec((length, 128), lambda i: (0, pair))
    return pl.pallas_call(
        forward_kernel,
        grid=(length // block,),
        in_specs=[pl.BlockSpec((block, 128), lambda i: (i, pair)), whole, whole],
        out_specs=[
            pl.BlockSpec((block, 128), lambda i: (i, 0)),
            pl.BlockSpec((1, 2, block), lambda i: (0, 0, i)),
        ],
        out_shape=[
            jax.ShapeDtypeStruct((length, 128), BF16),
            jax.ShapeDtypeStruct((1, 2, length), F32),
        ],
        scratch_shapes=[pltpu.VMEM((128, length), BF16)],
        compiler_params=pltpu.CompilerParams(vmem_limit_bytes=44 << 20),
        cost_estimate=pl.CostEstimate(
            flops=32 * length * length * HD,
            transcendentals=2 * length * length,
            bytes_accessed=8 * length * 128,
        ),
        name="attend_forward",
    )(query, keys, values)


def backward_kernel(
    q_ref, k_ref, v_ref, c_ref, g_ref, total_ref, dq_ref, dk_ref, dv_ref, sum_ref, inner_ref
):
    step = pl.program_id(0)

    @pl.when(step == 0)
    def _():
        product = g_ref[...].astype(F32) * c_ref[...].astype(F32)
        upper = product.astype(BF16)
        lower = (product - upper.astype(F32)).astype(BF16)
        row = lax.broadcasted_iota(jnp.int32, (8, 128), 0)
        column = lax.broadcasted_iota(jnp.int32, (8, 128), 1)
        pick = jnp.where(
            (column >= HD * row) & (column < HD * row + HD), 1.0, 0.0
        ).astype(BF16)
        inner_ref[...] = lax.dot_general(
            pick, upper, NT, preferred_element_type=F32
        ) + lax.dot_general(pick, lower, NT, preferred_element_type=F32)

    keys = k_ref[...] * jnp.asarray(0.125, BF16)
    values = v_ref[...]
    flipped = jnp.transpose(keys)
    lane = lax.broadcasted_iota(jnp.int32, keys.shape, 1)
    nothing = jnp.zeros_like(keys)
    value_grads, key_grads, query_grads = [], [], []
    for head in range(2):
        own = (lane >= HD * head) & (lane < HD * head + HD)
        scores = lax.dot_general(
            jnp.where(own, keys, nothing), q_ref[...], NT, preferred_element_type=F32
        )
        probs = jnp.exp(scores - total_ref[0, head : head + 1, :])
        value_grads.append(
            lax.dot_general(probs.astype(BF16), g_ref[...], NN, preferred_element_type=F32)
        )
        prob_grad = lax.dot_general(
            jnp.where(own, values, nothing), g_ref[...], NT, preferred_element_type=F32
        )
        score_grad = (probs * (prob_grad - inner_ref[head : head + 1, :])).astype(BF16)
        key_grads.append(
            lax.dot_general(score_grad, q_ref[...], NN, preferred_element_type=F32)
        )
        query_grads.append(
            lax.dot_general(
                flipped[HD * head : HD * head + HD, :],
                score_grad,
                NN,
                preferred_element_type=F32,
            )
        )
    first = lane < HD
    dk_ref[...] = (jnp.where(first, key_grads[0], key_grads[1]) * 0.125).astype(BF16)
    dv_ref[...] = jnp.where(first, value_grads[0], value_grads[1]).astype(BF16)
    query_grad = jnp.concatenate(query_grads, axis=0)

    @pl.when(step == 0)
    def _():
        sum_ref[...] = query_grad

    @pl.when(step > 0)
    def _():
        sum_ref[...] += query_grad

    @pl.when(step == pl.num_programs(0) - 1)
    def _():
        dq_ref[...] = jnp.transpose(sum_ref[...]).astype(BF16)


def attend_backward(query, keys, values, context, grad, totals, pair, block):
    length = query.shape[0]
    whole = pl.BlockSpec((length, 128), lambda j: (0, pair))
    part = pl.BlockSpec((block, 128), lambda j: (j, pair))
    single = pl.BlockSpec((length, 128), lambda j: (0, 0))
    out_part = pl.BlockSpec((block, 128), lambda j: (j, 0))
    return pl.pallas_call(
        backward_kernel,
        grid=(length // block,),
        in_specs=[
            whole,
            part,
            part,
            single,
            whole,
            pl.BlockSpec((1, 2, length), lambda j: (0, 0, 0)),
        ],
        out_specs=[single, out_part, out_part],
        out_shape=[jax.ShapeDtypeStruct((length, 128), BF16)] * 3,
        scratch_shapes=[pltpu.VMEM((128, length), F32), pltpu.VMEM((8, length), F32)],
        compiler_params=pltpu.CompilerParams(vmem_limit_bytes=48 << 20),
        cost_estimate=pl.CostEstimate(
            flops=80 * length * length * HD,
            transcendentals=2 * length * length,
            bytes_accessed=20 * length * 128,
        ),
        name="attend_backward",
    )(query, keys, values, context, grad, totals)


def swap(value, axis, mask, size):
    return lax.ppermute(value, axis, [(i, i ^ mask) for i in range(size)])


def bits_of(axis, size):
    mine = lax.axis_index(axis)
    count = size.bit_length() - 1
    return [(axis, 1 << b, size, (mine >> b) & 1) for b in reversed(range(count))]


def gather_bits(value, bits, order):
    held = []
    for place in order:
        axis, mask, size, bit = bits[place]
        other = swap(value, axis, mask, size)
        at = sum(1 for h in held if h < place)
        low = jnp.where(bit == 1, other, value)
        high = jnp.where(bit == 1, value, other)
        value = jnp.stack([low, high], axis=at)
        held.append(place)
    return value


def scatter_bits(value, bits, order, last=F32, wire=BF16):
    left = list(range(len(bits)))
    for place in order:
        axis, mask, size, bit = bits[place]
        at = left.index(place)
        away = lax.dynamic_index_in_dim(value, 1 - bit, at, keepdims=False).astype(wire)
        keep = lax.dynamic_index_in_dim(value, bit, at, keepdims=False)
        left.remove(place)
        value = keep.astype(F32) + swap(away, axis, mask, size).astype(F32)
        value = value.astype(wire if left else last)
    return value


def in_number_order(pieces, mine):
    pieces = list(pieces)
    step = 1
    while step < len(pieces):
        flip = (mine & step) != 0
        for i in range(len(pieces)):
            if not i & step:
                a, b = pieces[i], pieces[i | step]
                pieces[i] = jnp.where(flip, b, a)
                pieces[i | step] = jnp.where(flip, a, b)
        step *= 2
    return pieces


def gather_blocks(value, axis, size, masks):
    held = {0: value}
    for mask in masks:
        held.update({r ^ mask: swap(piece, axis, mask, size) for r, piece in list(held.items())})
    return held


def body(
    seqs,
    shards,
    layer_input,
    cotangent,
    weight_qkv,
    weight_merge,
    weight_expand,
    weight_shrink,
    norm_gains,
    all_biases,
    bias_hidden,
    moment_qkv,
    moment_merge,
    moment_expand,
    moment_shrink,
    moment_gains,
    moment_biases,
    moment_hidden,
    squares_qkv,
    squares_merge,
    squares_expand,
    squares_shrink,
    squares_gains,
    squares_biases,
    squares_hidden,
):
    params = (
        weight_qkv,
        weight_merge,
        weight_expand,
        weight_shrink,
        norm_gains,
        all_biases,
        bias_hidden,
    )
    moments = (
        moment_qkv,
        moment_merge,
        moment_expand,
        moment_shrink,
        moment_gains,
        moment_biases,
        moment_hidden,
    )
    squares = (
        squares_qkv,
        squares_merge,
        squares_expand,
        squares_shrink,
        squares_gains,
        squares_biases,
        squares_hidden,
    )
    devices = seqs * shards
    mine = lax.axis_index("seq")
    seq_bits = bits_of("seq", seqs)
    shard_bits = bits_of("shard", shards)
    bits = seq_bits + shard_bits
    ks, kh = len(seq_bits), len(shard_bits)
    core = ks + kh - 1
    far = [place for place in reversed(range(ks, core))]
    one_way = [core] + list(reversed(range(ks))) + far
    other_way = [core] + list(range(ks)) + far
    tokens = layer_input[0]
    count, width = tokens.shape
    local = width // seqs
    pairs = local // 128
    hidden_width = bias_hidden.shape[0] * devices
    part = norm_gains.shape[1]

    small = jnp.concatenate(
        [
            norm_gains.astype(BF16).reshape(-1),
            all_biases.astype(BF16).reshape(-1),
            bias_hidden.astype(BF16),
        ]
    )
    small = gather_bits(small[None], bits, list(range(len(bits))))
    small = small.reshape(devices, 8 * part + bias_hidden.shape[0]).astype(F32)
    rows = small[:, : 8 * part].reshape(devices, 8, part).transpose(1, 0, 2).reshape(8, width)
    gains, biases = rows[:2], rows[2:]
    hidden_bias = small[:, 8 * part :].reshape(hidden_width)

    by_heads = weight_qkv.astype(BF16).reshape(-1, 3, seqs, local)
    columns = [
        swap(lax.dynamic_index_in_dim(by_heads, mine ^ r, 2, keepdims=False), "seq", r, seqs)
        if r
        else lax.dynamic_index_in_dim(by_heads, mine, 2, keepdims=False)
        for r in range(seqs)
    ]
    columns = jnp.stack(in_number_order(columns, mine))
    columns = columns.reshape(seqs, -1, 3 * local)
    for place in range(kh):
        axis, mask, size, bit = shard_bits[place]
        other = swap(columns, axis, mask, size)
        columns = jnp.stack(
            [jnp.where(bit == 1, other, columns), jnp.where(bit == 1, columns, other)],
            axis=1 + place,
        )
    own_qkv = columns.reshape(width, 3 * local)

    half = count // 2
    masks = [1 << b for b in range(ks)]
    upper = gather_blocks(tokens[:half], "seq", seqs, masks)
    lower = gather_blocks(tokens[half:], "seq", seqs, masks[::-1])
    every = jnp.concatenate(
        [piece for r in range(seqs) for piece in (upper[r], lower[r])], axis=0
    )

    full_merge = gather_bits(
        weight_merge.astype(BF16), bits, list(range(ks, core)) + list(range(ks)) + [core]
    ).reshape(width, width)
    full_expand = lax.all_gather(weight_expand.astype(BF16), ("seq", "shard"), axis=0, tiled=True)
    full_shrink = lax.all_gather(weight_shrink.astype(BF16), ("seq", "shard"), axis=0, tiled=True)

    own_bias = lax.dynamic_slice_in_dim(biases[1:3], mine * local, local, 1)
    bias_row = jnp.concatenate([own_bias[0], jnp.zeros((local,), F32), own_bias[1]])
    qkv = (jnp.dot(every, own_qkv, preferred_element_type=F32) + bias_row).astype(BF16)
    query, keys, values = qkv[:, :local], qkv[:, local : 2 * local], qkv[:, 2 * local :]
    length = qkv.shape[0]
    block = min(512, length)
    contexts, totals, arrived = [], [], []
    for pair in range(pairs):
        context_pair, total = attend_forward(query, keys, values, pair, block)
        contexts.append(context_pair)
        totals.append(total)
        arrived.append(
            in_number_order(
                [
                    swap(context_pair[r * count : (r + 1) * count], "seq", r, seqs)
                    if r
                    else context_pair[:count]
                    for r in range(seqs)
                ],
                mine,
            )
        )
    context = jnp.concatenate(
        [arrived[pair][s] for s in range(seqs) for pair in range(pairs)], axis=1
    )

    attended = jnp.dot(context, full_merge, preferred_element_type=F32) + biases[3]
    first, normed_one, inverse_one = norm_forward(
        tokens.astype(F32) + attended, gains[0], biases[0]
    )
    first_low = first.astype(BF16)
    hidden = jnp.dot(first_low, full_expand, preferred_element_type=F32) + hidden_bias
    active = jax.nn.gelu(hidden, approximate=False).astype(BF16)
    branch = jnp.dot(active, full_shrink, preferred_element_type=F32) + biases[5]
    result, normed_two, inverse_two = norm_forward(first + branch, gains[1], biases[4])
    grad_out = cotangent[0]
    grad_gain_two = jnp.sum(grad_out * normed_two, axis=0)
    grad_shift_two = jnp.sum(grad_out, axis=0)
    grad_mid = norm_backward(grad_out, normed_two, inverse_two, gains[1])
    grad_branch = grad_mid.astype(BF16)
    grad_shrink_bias = jnp.sum(grad_branch, axis=0, dtype=F32)

    def summed_weight(left, right):
        middle = right.shape[1] // 2
        parts = []
        for piece, order in ((right[:, :middle], one_way), (right[:, middle:], other_way)):
            grad = lax.dot_general(left, piece, TN, preferred_element_type=F32).astype(BF16)
            grad = grad.reshape((2,) * len(bits) + (-1, middle))
            parts.append(scatter_bits(grad, bits, order))
        return jnp.concatenate(parts, axis=1)

    summed_shrink = summed_weight(active, grad_branch)
    grad_active = lax.dot_general(grad_branch, full_shrink, NT, preferred_element_type=F32)
    grad_hidden = (grad_active * gelu_slope(hidden)).astype(BF16)
    grad_hidden_bias = jnp.sum(grad_hidden, axis=0, dtype=F32)
    summed_expand = summed_weight(first_low, grad_hidden)
    grad_first = grad_mid + lax.dot_general(
        grad_hidden, full_expand, NT, preferred_element_type=F32
    )
    grad_gain_one = jnp.sum(grad_first * normed_one, axis=0)
    grad_shift_one = jnp.sum(grad_first, axis=0)
    grad_residual = norm_backward(grad_first, normed_one, inverse_one, gains[0])
    grad_attended = grad_residual.astype(BF16)
    grad_merge_bias = jnp.sum(grad_attended, axis=0, dtype=F32)
    grad_heads = lax.dot_general(
        grad_attended, full_merge, NT, preferred_element_type=F32
    ).astype(BF16)
    grad_context = jnp.concatenate(
        [
            swap(lax.dynamic_slice_in_dim(grad_heads, (mine ^ r) * local, local, 1), "seq", r, seqs)
            if r
            else lax.dynamic_slice_in_dim(grad_heads, mine * local, local, 1)
            for r in range(seqs)
        ],
        axis=0,
    )
    summed_merge = summed_weight(context, grad_attended)

    small_grads = jnp.concatenate(
        [
            jnp.stack(
                [
                    grad_gain_one,
                    grad_gain_two,
                    grad_shift_one,
                    grad_merge_bias,
                    grad_shift_two,
                    grad_shrink_bias,
                ]
            )
            .reshape(6, devices, part)
            .transpose(1, 0, 2)
            .reshape(devices, 6 * part),
            grad_hidden_bias.reshape(devices, -1),
        ],
        axis=1,
    )
    small_grads = scatter_bits(
        small_grads.reshape((2,) * len(bits) + (1, -1)), bits, list(range(len(bits))), F32, F32
    )[0]

    grads = [
        attend_backward(
            query, keys, values, contexts[pair], grad_context, totals[pair], pair, block
        )
        for pair in range(pairs)
    ]
    grad_rows = jnp.concatenate(
        [grads[pair][which] for which in range(3) for pair in range(pairs)], axis=1
    )
    grad_weight = lax.dot_general(every, grad_rows, TN, preferred_element_type=F32).astype(BF16)
    grad_weight = grad_weight.reshape((seqs,) + (2,) * kh + (-1, 3 * local))
    for turn, place in enumerate(reversed(range(kh))):
        axis, mask, size, bit = shard_bits[place]
        away = lax.dynamic_index_in_dim(grad_weight, 1 - bit, 1 + place, keepdims=False)
        keep = lax.dynamic_index_in_dim(grad_weight, bit, 1 + place, keepdims=False)
        grad_weight = (
            keep.astype(F32) + swap(away, axis, mask, size).astype(F32)
        ).astype(BF16)
    summed_qkv = in_number_order(
        [
            swap(lax.dynamic_index_in_dim(grad_weight, mine ^ r, 0, keepdims=False), "seq", r, seqs)
            if r
            else lax.dynamic_index_in_dim(grad_weight, mine, 0, keepdims=False)
            for r in range(seqs)
        ],
        mine,
    )
    summed_qkv = (
        jnp.stack([piece.reshape(-1, 3, local) for piece in summed_qkv], axis=2)
        .reshape(-1, 3 * width)
        .astype(F32)
    )
    head_sums = jnp.stack(
        [
            jnp.sum(grad_rows[:, :local], axis=0, dtype=F32).reshape(shards, part),
            jnp.sum(grad_rows[:, 2 * local :], axis=0, dtype=F32).reshape(shards, part),
        ],
        axis=1,
    )
    head_sums = scatter_bits(
        head_sums.reshape((2,) * kh + (2, part)), shard_bits, list(range(kh)), F32, F32
    )
    spread = lax.dot_general(grad_rows, own_qkv, NT, preferred_element_type=F32)
    grad_input = grad_residual + spread[:count]
    for r in range(1, seqs):
        away = spread[r * count : (r + 1) * count].astype(BF16)
        grad_input = grad_input + swap(away, "seq", r, seqs).astype(F32)

    small_rows = small_grads[: 6 * part].reshape(6, part)
    summed = (
        summed_qkv,
        summed_merge,
        summed_expand,
        summed_shrink,
        small_rows[:2],
        jnp.concatenate([small_rows[2:3], head_sums, small_rows[3:]], axis=0),
        small_grads[6 * part :],
    )
    finals = []
    momenta = []
    squared_all = []
    for index in range(7):
        master, change, momentum, squared = adam_update(
            params[index], summed[index], moments[index], squares[index], index < 4
        )
        finals.append(master if index < 4 else change)
        momenta.append(momentum)
        squared_all.append(squared)
    layer_output = result.astype(BF16)[None]
    return (
        (layer_output, grad_input[None])
        + summed
        + tuple(finals)
        + tuple(momenta)
        + tuple(squared_all)
    )


def solution(mesh):
    both = ("seq", "shard")
    rows, columns, flat = P(both, None), P(None, both), P(both)
    group = (rows, rows, rows, rows, columns, columns, flat)
    states = P("shard", "seq", None)
    return jax.shard_map(
        functools.partial(body, mesh.shape["seq"], mesh.shape["shard"]),
        mesh=mesh,
        in_specs=(states, states) + group * 3,
        out_specs=(states, states) + group * 4,
        check_vma=False,
    )
```

```python
import functools

import jax
import jax.numpy as jnp
from jax import lax
from jax.experimental import pallas as pl
from jax.experimental.pallas import tpu as pltpu
from jax.sharding import PartitionSpec as P

HD = 64
STEP = 10
F32 = jnp.float32
BF16 = jnp.bfloat16
NT = (((1,), (1,)), ((), ()))
NN = (((1,), (0,)), ((), ()))
TN = (((0,), (0,)), ((), ()))


def norm_forward(value, gain, shift):
    centre = value - jnp.mean(value, axis=-1, keepdims=True)
    inverse = lax.rsqrt(jnp.mean(centre * centre, axis=-1, keepdims=True) + 1e-06)
    normed = centre * inverse
    return (normed * gain + shift, normed, inverse)


def norm_backward(grad, normed, inverse, gain):
    scaled = grad * gain
    inner = jnp.mean(scaled * normed, axis=-1, keepdims=True)
    return inverse * (scaled - jnp.mean(scaled, axis=-1, keepdims=True) - normed * inner)


def normal_share(hidden):
    return 0.5 * (1.0 + lax.erf(hidden * 0.7071067811865476))


def gelu_slope(hidden):
    return normal_share(hidden) + hidden * jnp.exp(-0.5 * hidden * hidden) * 0.3989422804014327


def adam_update(param, grad, moment, squares, decay):
    momentum = 0.9 * moment + 0.1 * grad
    squared = 0.999 * squares + 0.001 * grad * grad
    update = momentum / (1.0 - 0.9**STEP) / (jnp.sqrt(squared / (1.0 - 0.999**STEP)) + 1e-08)
    if decay:
        update = update + 0.01 * param
    change = -0.02 * update
    return (param - 0.02 * update, change, momentum, squared)


def forward_kernel(q_ref, k_ref, v_ref, c_ref, total_ref, flipped_ref):
    @pl.when(pl.program_id(0) == 0)
    def _():
        flipped_ref[...] = jnp.transpose(v_ref[...])

    query = q_ref[...] * jnp.asarray(0.125, BF16)
    lane = lax.broadcasted_iota(jnp.int32, query.shape, 1)
    pieces, rows = [], []
    for head in range(2):
        own = (lane >= HD * head) & (lane < HD * head + HD)
        scores = lax.dot_general(
            k_ref[...], jnp.where(own, query, jnp.zeros_like(query)), NT, preferred_element_type=F32
        )
        highest = jnp.max(scores, axis=0, keepdims=True)
        weights = jnp.exp(scores - highest)
        total = jnp.sum(weights, axis=0, keepdims=True)
        context = lax.dot_general(
            flipped_ref[HD * head : HD * head + HD, :],
            weights.astype(BF16),
            NN,
            preferred_element_type=F32,
        )
        pieces.append(context * (1.0 / total))
        rows.append(highest + jnp.log(total))
    c_ref[...] = jnp.transpose(jnp.concatenate(pieces, axis=0)).astype(BF16)
    total_ref[...] = jnp.concatenate(rows, axis=0)[None]


def attend_forward(query, keys, values, pair, block):
    length = query.shape[0]
    whole = pl.BlockSpec((length, 128), lambda i: (0, pair))
    return pl.pallas_call(
        forward_kernel,
        grid=(length // block,),
        in_specs=[pl.BlockSpec((block, 128), lambda i: (i, pair)), whole, whole],
        out_specs=[
            pl.BlockSpec((block, 128), lambda i: (i, 0)),
            pl.BlockSpec((1, 2, block), lambda i: (0, 0, i)),
        ],
        out_shape=[
            jax.ShapeDtypeStruct((length, 128), BF16),
            jax.ShapeDtypeStruct((1, 2, length), F32),
        ],
        scratch_shapes=[pltpu.VMEM((128, length), BF16)],
        compiler_params=pltpu.CompilerParams(vmem_limit_bytes=44 << 20),
        cost_estimate=pl.CostEstimate(
            flops=32 * length * length * HD,
            transcendentals=2 * length * length,
            bytes_accessed=8 * length * 128,
        ),
        name="attend_forward",
    )(query, keys, values)


def backward_kernel(
    q_ref, k_ref, v_ref, c_ref, g_ref, total_ref, dq_ref, dk_ref, dv_ref, sum_ref, inner_ref
):
    step = pl.program_id(0)

    @pl.when(step == 0)
    def _():
        product = g_ref[...].astype(F32) * c_ref[...].astype(F32)
        upper = product.astype(BF16)
        lower = (product - upper.astype(F32)).astype(BF16)
        row = lax.broadcasted_iota(jnp.int32, (8, 128), 0)
        column = lax.broadcasted_iota(jnp.int32, (8, 128), 1)
        pick = jnp.where(
            (column >= HD * row) & (column < HD * row + HD), 1.0, 0.0
        ).astype(BF16)
        inner_ref[...] = lax.dot_general(
            pick, upper, NT, preferred_element_type=F32
        ) + lax.dot_general(pick, lower, NT, preferred_element_type=F32)

    keys = k_ref[...] * jnp.asarray(0.125, BF16)
    values = v_ref[...]
    flipped = jnp.transpose(keys)
    lane = lax.broadcasted_iota(jnp.int32, keys.shape, 1)
    nothing = jnp.zeros_like(keys)
    value_grads, key_grads, query_grads = [], [], []
    for head in range(2):
        own = (lane >= HD * head) & (lane < HD * head + HD)
        scores = lax.dot_general(
            jnp.where(own, keys, nothing), q_ref[...], NT, preferred_element_type=F32
        )
        probs = jnp.exp(scores - total_ref[0, head : head + 1, :])
        value_grads.append(
            lax.dot_general(probs.astype(BF16), g_ref[...], NN, preferred_element_type=F32)
        )
        prob_grad = lax.dot_general(
            jnp.where(own, values, nothing), g_ref[...], NT, preferred_element_type=F32
        )
        score_grad = (probs * (prob_grad - inner_ref[head : head + 1, :])).astype(BF16)
        key_grads.append(
            lax.dot_general(score_grad, q_ref[...], NN, preferred_element_type=F32)
        )
        query_grads.append(
            lax.dot_general(
                flipped[HD * head : HD * head + HD, :],
                score_grad,
                NN,
                preferred_element_type=F32,
            )
        )
    first = lane < HD
    dk_ref[...] = (jnp.where(first, key_grads[0], key_grads[1]) * 0.125).astype(BF16)
    dv_ref[...] = jnp.where(first, value_grads[0], value_grads[1]).astype(BF16)
    query_grad = jnp.concatenate(query_grads, axis=0)

    @pl.when(step == 0)
    def _():
        sum_ref[...] = query_grad

    @pl.when(step > 0)
    def _():
        sum_ref[...] += query_grad

    @pl.when(step == pl.num_programs(0) - 1)
    def _():
        dq_ref[...] = jnp.transpose(sum_ref[...]).astype(BF16)


def attend_backward(query, keys, values, context, grad, totals, pair, block):
    length = query.shape[0]
    whole = pl.BlockSpec((length, 128), lambda j: (0, pair))
    part = pl.BlockSpec((block, 128), lambda j: (j, pair))
    single = pl.BlockSpec((length, 128), lambda j: (0, 0))
    out_part = pl.BlockSpec((block, 128), lambda j: (j, 0))
    return pl.pallas_call(
        backward_kernel,
        grid=(length // block,),
        in_specs=[
            whole,
            part,
            part,
            single,
            whole,
            pl.BlockSpec((1, 2, length), lambda j: (0, 0, 0)),
        ],
        out_specs=[single, out_part, out_part],
        out_shape=[jax.ShapeDtypeStruct((length, 128), BF16)] * 3,
        scratch_shapes=[pltpu.VMEM((128, length), F32), pltpu.VMEM((8, length), F32)],
        compiler_params=pltpu.CompilerParams(vmem_limit_bytes=48 << 20),
        cost_estimate=pl.CostEstimate(
            flops=80 * length * length * HD,
            transcendentals=2 * length * length,
            bytes_accessed=20 * length * 128,
        ),
        name="attend_backward",
    )(query, keys, values, context, grad, totals)


def swap(value, axis, mask, size):
    return lax.ppermute(value, axis, [(i, i ^ mask) for i in range(size)])


def bits_of(axis, size):
    mine = lax.axis_index(axis)
    count = size.bit_length() - 1
    return [(axis, 1 << b, size, (mine >> b) & 1) for b in reversed(range(count))]


def split(value, bit, at):
    keep = lax.dynamic_index_in_dim(value, bit, at, keepdims=False)
    away = lax.dynamic_index_in_dim(value, 1 - bit, at, keepdims=False)
    return keep, away


def add(*values, dtype=BF16):
    total = values[0].astype(F32)
    for value in values[1:]:
        total = total + value.astype(F32)
    return total.astype(dtype)


def hold(value, *others):
    return lax.optimization_barrier((value,) + others)[0]


def in_number_order(pieces, mine):
    pieces = list(pieces)
    step = 1
    while step < len(pieces):
        flip = (mine & step) != 0
        for i in range(len(pieces)):
            if not i & step:
                a, b = pieces[i], pieces[i | step]
                pieces[i] = jnp.where(flip, b, a)
                pieces[i | step] = jnp.where(flip, a, b)
        step *= 2
    return pieces


def gather_blocks(value, axis, size, masks):
    held = {0: value}
    for mask in masks:
        held.update({r ^ mask: swap(piece, axis, mask, size) for r, piece in list(held.items())})
    return held


def gather_direct(value, axis, size, step=1):
    mine = lax.axis_index(axis) // step
    pieces = [value] + [swap(value, axis, r, size) for r in range(step, size, step)]
    return jnp.stack(in_number_order(pieces, mine))


def gather_core(value, size, at):
    other = swap(value, "shard", 1, size)
    bit = lax.axis_index("shard") & 1
    low = jnp.where(bit == 1, other, value)
    high = jnp.where(bit == 1, value, other)
    return jnp.stack([low, high], axis=at)


def scatter_direct(value, axis, size, step=1):
    mine = lax.axis_index(axis) // step
    parts = [lax.dynamic_index_in_dim(value, mine, 0, keepdims=False)]
    for r in range(1, size // step):
        away = lax.dynamic_index_in_dim(value, mine ^ r, 0, keepdims=False)
        parts.append(swap(away, axis, r * step, size))
    return parts


def body(
    seqs,
    shards,
    layer_input,
    cotangent,
    weight_qkv,
    weight_merge,
    weight_expand,
    weight_shrink,
    norm_gains,
    all_biases,
    bias_hidden,
    moment_qkv,
    moment_merge,
    moment_expand,
    moment_shrink,
    moment_gains,
    moment_biases,
    moment_hidden,
    squares_qkv,
    squares_merge,
    squares_expand,
    squares_shrink,
    squares_gains,
    squares_biases,
    squares_hidden,
):
    params = (
        weight_qkv,
        weight_merge,
        weight_expand,
        weight_shrink,
        norm_gains,
        all_biases,
        bias_hidden,
    )
    moments = (
        moment_qkv,
        moment_merge,
        moment_expand,
        moment_shrink,
        moment_gains,
        moment_biases,
        moment_hidden,
    )
    squares = (
        squares_qkv,
        squares_merge,
        squares_expand,
        squares_shrink,
        squares_gains,
        squares_biases,
        squares_hidden,
    )
    devices = seqs * shards
    far = shards // 2
    mine = lax.axis_index("seq")
    core = lax.axis_index("shard") & 1
    masks = [1 << b for b in range(seqs.bit_length() - 1)]
    tokens = layer_input[0]
    count, width = tokens.shape
    half = count // 2
    local = width // seqs
    pairs = local // 128
    hidden_width = bias_hidden.shape[0] * devices
    part = norm_gains.shape[1]

    by_heads = weight_qkv.astype(BF16).reshape(-1, 3, seqs, local)
    by_heads = by_heads.transpose(2, 0, 1, 3).reshape(seqs, -1, 3 * local)
    own_qkv = jnp.stack(in_number_order(scatter_direct(by_heads, "seq", seqs), mine))

    upper = gather_blocks(tokens[:half], "seq", seqs, masks)
    lower = gather_blocks(tokens[half:], "seq", seqs, masks[::-1])

    each = own_qkv.shape[0] * own_qkv.shape[1]
    own_bias = all_biases[1:3].astype(BF16).reshape(1, 2 * part)
    own_qkv = jnp.concatenate(
        [
            own_qkv.reshape(each, 3 * local),
            jnp.pad(own_bias, ((0, 7), (0, 3 * local - 2 * part))),
        ],
        axis=0,
    )
    own_qkv = gather_direct(own_qkv, "shard", shards, 2)
    own_qkv = gather_core(own_qkv, shards, 1)
    own_bias = own_qkv[:, :, each, : 2 * part].astype(F32).reshape(shards, 2, part)
    own_bias = own_bias.transpose(1, 0, 2).reshape(2, local)
    own_qkv = own_qkv[:, :, :each].reshape(far, 2, seqs, -1, 3 * local)
    own_qkv = own_qkv.transpose(2, 0, 1, 3, 4).reshape(width, 3 * local)

    deep = weight_expand.shape[0]
    small = jnp.concatenate(
        [
            norm_gains.astype(BF16).reshape(-1),
            all_biases.astype(BF16).reshape(-1),
            bias_hidden.astype(BF16),
        ]
    ).reshape(deep, -1)
    thin = small.shape[1]
    mixed = jnp.concatenate(
        [
            weight_expand.astype(BF16),
            weight_merge.astype(BF16),
            jnp.pad(small, ((0, 0), (0, 128 - thin))),
        ],
        axis=1,
    )
    mixed = lax.all_gather(mixed, ("seq", "shard"), axis=0, tiled=True)
    full_expand = mixed[:, :hidden_width]
    full_merge = mixed[:, hidden_width : hidden_width + width]
    small = mixed[:, hidden_width + width :][:, :thin].reshape(devices, -1).astype(F32)
    rows = small[:, : 8 * part].reshape(devices, 8, part).transpose(1, 0, 2).reshape(8, width)
    gains, biases = rows[:2], rows[2:]
    hidden_bias = small[:, 8 * part :].reshape(hidden_width)

    every = jnp.concatenate(
        [piece for r in range(seqs) for piece in (upper[r], lower[r])], axis=0
    )
    full_shrink = lax.all_gather(weight_shrink.astype(BF16), ("seq", "shard"), axis=0, tiled=True)

    bias_row = jnp.concatenate([own_bias[0], jnp.zeros((local,), F32), own_bias[1]])
    qkv = (jnp.dot(every, own_qkv, preferred_element_type=F32) + bias_row).astype(BF16)
    query, keys, values = qkv[:, :local], qkv[:, local : 2 * local], qkv[:, 2 * local :]
    length = qkv.shape[0]
    block = min(512, length)
    contexts, totals, arrived = [], [], []
    for pair in range(pairs):
        context_pair, total = attend_forward(query, keys, values, pair, block)
        contexts.append(context_pair)
        totals.append(total)
        arrived.append(
            in_number_order(
                [
                    swap(context_pair[r * count : (r + 1) * count], "seq", r, seqs)
                    if r
                    else context_pair[:count]
                    for r in range(seqs)
                ],
                mine,
            )
        )
    context = jnp.concatenate(
        [arrived[pair][s] for s in range(seqs) for pair in range(pairs)], axis=1
    )

    attended = jnp.dot(context, full_merge, preferred_element_type=F32) + biases[3]
    first, normed_one, inverse_one = norm_forward(
        tokens.astype(F32) + attended, gains[0], biases[0]
    )
    first_low = first.astype(BF16)
    hidden = jnp.dot(first_low, full_expand, preferred_element_type=F32) + hidden_bias
    active = (hidden * normal_share(hidden)).astype(BF16)
    branch = jnp.dot(active, full_shrink, preferred_element_type=F32) + biases[5]
    result, normed_two, inverse_two = norm_forward(first + branch, gains[1], biases[4])
    grad_out = cotangent[0]
    grad_gain_two = jnp.sum(grad_out * normed_two, axis=0)
    grad_shift_two = jnp.sum(grad_out, axis=0)
    grad_mid = norm_backward(grad_out, normed_two, inverse_two, gains[1])
    grad_branch = grad_mid.astype(BF16)
    grad_shrink_bias = jnp.sum(grad_branch, axis=0, dtype=F32)

    def core_step(left, right, extra=None):
        grad = lax.dot_general(left, right, TN, preferred_element_type=F32).astype(BF16)
        grad = grad.reshape(seqs, far, 2, -1, grad.shape[1])
        if extra is not None:
            grad = jnp.concatenate([grad, extra], axis=-1)
        keep, away = split(grad, core, 2)
        return keep, swap(away, "shard", 1, shards), away

    def halving_start(grad, way):
        grad = grad.reshape((2,) * len(masks) + grad.shape[1:])
        return halving_send(grad, masks[::-1], way)

    def halving_send(grad, left, way):
        mask = way[0]
        keep, away = split(grad, (mine // mask) & 1, left.index(mask))
        left = [m for m in left if m != mask]
        return keep, swap(away, "seq", mask, seqs), away, left, way[1:]

    def halving_next(started, *others):
        if not isinstance(started, tuple):
            return started
        keep, got, _, left, way = started
        grad = add(keep, hold(got, *others))
        return halving_send(grad, left, way) if way else grad

    grad_shrink = lax.dot_general(active, grad_branch, TN, preferred_element_type=F32).astype(BF16)
    summed_shrink = lax.psum_scatter(
        grad_shrink, ("seq", "shard"), scatter_dimension=0, tiled=True
    ).astype(F32)
    grad_branch = hold(grad_branch, grad_shrink)
    grad_active = lax.dot_general(grad_branch, full_shrink, NT, preferred_element_type=F32)
    grad_hidden = (grad_active * gelu_slope(hidden)).astype(BF16)
    grad_hidden_bias = jnp.sum(grad_hidden, axis=0, dtype=F32)
    expand_keep, expand_got, away = core_step(first_low, grad_hidden)
    grad_hidden = hold(grad_hidden, away)
    grad_first = grad_mid + lax.dot_general(
        grad_hidden, full_expand, NT, preferred_element_type=F32
    )
    grad_gain_one = jnp.sum(grad_first * normed_one, axis=0)
    grad_shift_one = jnp.sum(grad_first, axis=0)
    grad_residual = norm_backward(grad_first, normed_one, inverse_one, gains[0])
    grad_attended = grad_residual.astype(BF16)
    grad_merge_bias = jnp.sum(grad_attended, axis=0, dtype=F32)
    grad_heads = lax.dot_general(
        grad_attended, full_merge, NT, preferred_element_type=F32
    ).astype(BF16)
    grad_heads = grad_heads.reshape(count, seqs, local).transpose(1, 0, 2)
    grad_context = jnp.concatenate(scatter_direct(grad_heads, "seq", seqs), axis=0)
    small_grads = jnp.concatenate(
        [
            jnp.stack(
                [
                    grad_gain_one,
                    grad_gain_two,
                    grad_shift_one,
                    grad_merge_bias,
                    grad_shift_two,
                    grad_shrink_bias,
                ]
            )
            .reshape(6, devices, part)
            .transpose(1, 0, 2)
            .reshape(devices, 6 * part),
            grad_hidden_bias.reshape(devices, -1),
        ],
        axis=1,
    )
    small_grads = small_grads.astype(BF16).reshape(seqs, far, 2, deep, -1)
    slim = small_grads.shape[-1]
    small_grads = jnp.pad(small_grads, ((0, 0),) * 4 + ((0, 128 - slim),))
    merge_keep, merge_got, away = core_step(context, grad_attended, small_grads)

    expand = add(expand_keep, hold(expand_got, grad_context))
    middle = expand.shape[-1] // 2
    expand = [
        halving_start(expand[..., :middle], masks),
        halving_start(expand[..., middle:], masks[::-1]),
    ]
    grad_context = hold(grad_context, away, *[part[2] for part in expand])

    grads = []
    for pair in range(pairs):
        grads.append(
            attend_backward(
                query, keys, values, contexts[pair], grad_context, totals[pair], pair, block
            )
        )
        if pair == 0:
            merge = halving_start(add(merge_keep, hold(merge_got, grads[0][0])), masks)
            expand = [halving_next(part, grads[0][0]) for part in expand]
            grad_context = hold(grad_context, merge[2], *[part[2] for part in expand])
    last = grads[-1][0]
    while isinstance(merge, tuple):
        merge = halving_next(merge, last)
        expand = [halving_next(part, last) for part in expand]
    grad_rows = jnp.concatenate(
        [grads[pair][which] for which in range(3) for pair in range(pairs)], axis=1
    )

    spread = lax.dot_general(grad_rows, own_qkv, NT, preferred_element_type=F32).astype(BF16)
    spread = spread.reshape((2,) * len(masks) + (2, half, width))
    sides = []
    for side, way in ((0, masks), (1, masks[::-1])):
        held = lax.index_in_dim(spread, side, len(masks), keepdims=False)
        left = masks[::-1]
        for mask in way:
            at = left.index(mask)
            left = [m for m in left if m != mask]
            held = add(
                lax.index_in_dim(held, 0, at, keepdims=False),
                swap(lax.index_in_dim(held, 1, at, keepdims=False), "seq", mask, seqs),
                dtype=BF16 if left else F32,
            )
        sides.append(held)
    grad_input = grad_residual + jnp.concatenate(sides, axis=0)

    head_sums = jnp.stack(
        [
            jnp.sum(grad_rows[:, :local], axis=0, dtype=F32).reshape(shards, part),
            jnp.sum(grad_rows[:, 2 * local :], axis=0, dtype=F32).reshape(shards, part),
        ],
        axis=1,
    )
    head_sums = head_sums.astype(BF16).reshape(1, far, 2, deep, 2)
    head_sums = jnp.broadcast_to(
        jnp.pad(head_sums, ((0, 0),) * 4 + ((0, 126),)), (seqs, far, 2, deep, 128)
    )
    keep, got, _ = core_step(every, grad_rows, head_sums)
    grad_weight = add(keep, got).transpose(1, 0, 2, 3)
    grad_weight = add(*scatter_direct(grad_weight, "shard", shards, 2))
    arrived = scatter_direct(grad_weight, "seq", seqs)
    head_sums = arrived[0][:, 3 * local : 3 * local + 2].astype(F32).reshape(2, part)
    summed_qkv = in_number_order([piece[:, : 3 * local] for piece in arrived], mine)
    summed_qkv = (
        jnp.stack([piece.reshape(-1, 3, local) for piece in summed_qkv], axis=2)
        .reshape(-1, 3 * width)
        .astype(F32)
    )

    others = jnp.concatenate(expand + [merge], axis=-1)
    others = add(*scatter_direct(others, "shard", shards, 2), dtype=F32)
    summed_expand = others[:, :hidden_width]
    summed_merge = others[:, hidden_width : hidden_width + width]
    small_grads = others[:, hidden_width + width :][:, :slim].reshape(-1)

    small_rows = small_grads[: 6 * part].reshape(6, part)
    summed = (
        summed_qkv,
        summed_merge,
        summed_expand,
        summed_shrink,
        small_rows[:2],
        jnp.concatenate([small_rows[2:3], head_sums, small_rows[3:]], axis=0),
        small_grads[6 * part :],
    )
    finals = []
    momenta = []
    squared_all = []
    for index in range(7):
        master, change, momentum, squared = adam_update(
            params[index], summed[index], moments[index], squares[index], index < 4
        )
        finals.append(master if index < 4 else change)
        momenta.append(momentum)
        squared_all.append(squared)
    layer_output = result.astype(BF16)[None]
    return (
        (layer_output, grad_input[None])
        + summed
        + tuple(finals)
        + tuple(momenta)
        + tuple(squared_all)
    )


def solution(mesh):
    both = ("seq", "shard")
    rows, columns, flat = P(both, None), P(None, both), P(both)
    group = (rows, rows, rows, rows, columns, columns, flat)
    states = P("shard", "seq", None)
    return jax.shard_map(
        functools.partial(body, mesh.shape["seq"], mesh.shape["shard"]),
        mesh=mesh,
        in_specs=(states, states) + group * 3,
        out_specs=(states, states) + group * 4,
        check_vma=False,
    )
```

```python
import functools

import jax
import jax.numpy as jnp
from jax import lax
from jax.experimental import pallas as pl
from jax.experimental.pallas import tpu as pltpu
from jax.sharding import PartitionSpec as P

HD = 64
STEP = 10
F32 = jnp.float32
BF16 = jnp.bfloat16
NT = (((1,), (1,)), ((), ()))
NN = (((1,), (0,)), ((), ()))
TN = (((0,), (0,)), ((), ()))


def norm_forward(value, gain, shift):
    centre = value - jnp.mean(value, axis=-1, keepdims=True)
    inverse = lax.rsqrt(jnp.mean(centre * centre, axis=-1, keepdims=True) + 1e-06)
    normed = centre * inverse
    return (normed * gain + shift, normed, inverse)


def norm_backward(grad, normed, inverse, gain):
    scaled = grad * gain
    inner = jnp.mean(scaled * normed, axis=-1, keepdims=True)
    return inverse * (scaled - jnp.mean(scaled, axis=-1, keepdims=True) - normed * inner)


def normal_share(hidden):
    return 0.5 * (1.0 + lax.erf(hidden * 0.7071067811865476))


def gelu_slope(hidden):
    return normal_share(hidden) + hidden * jnp.exp(-0.5 * hidden * hidden) * 0.3989422804014327


def adam_update(param, grad, moment, squares, decay):
    momentum = 0.9 * moment + 0.1 * grad
    squared = 0.999 * squares + 0.001 * grad * grad
    update = momentum / (1.0 - 0.9**STEP) / (jnp.sqrt(squared / (1.0 - 0.999**STEP)) + 1e-08)
    if decay:
        update = update + 0.01 * param
    change = -0.02 * update
    return (param - 0.02 * update, change, momentum, squared)


def forward_kernel(q_ref, k_ref, v_ref, c_ref, total_ref, flipped_ref):
    @pl.when(pl.program_id(0) == 0)
    def _():
        flipped_ref[...] = jnp.transpose(v_ref[...])

    query = q_ref[...] * jnp.asarray(0.125, BF16)
    lane = lax.broadcasted_iota(jnp.int32, query.shape, 1)
    pieces, rows = [], []
    for head in range(2):
        own = (lane >= HD * head) & (lane < HD * head + HD)
        scores = lax.dot_general(
            k_ref[...], jnp.where(own, query, jnp.zeros_like(query)), NT, preferred_element_type=F32
        )
        highest = jnp.max(scores, axis=0, keepdims=True)
        weights = jnp.exp(scores - highest)
        total = jnp.sum(weights, axis=0, keepdims=True)
        context = lax.dot_general(
            flipped_ref[HD * head : HD * head + HD, :],
            weights.astype(BF16),
            NN,
            preferred_element_type=F32,
        )
        pieces.append(context * (1.0 / total))
        rows.append(highest + jnp.log(total))
    c_ref[...] = jnp.transpose(jnp.concatenate(pieces, axis=0)).astype(BF16)
    total_ref[...] = jnp.concatenate(rows, axis=0)[None]


def attend_forward(query, keys, values, pair, block):
    length = query.shape[0]
    whole = pl.BlockSpec((length, 128), lambda i: (0, pair))
    return pl.pallas_call(
        forward_kernel,
        grid=(length // block,),
        in_specs=[pl.BlockSpec((block, 128), lambda i: (i, pair)), whole, whole],
        out_specs=[
            pl.BlockSpec((block, 128), lambda i: (i, 0)),
            pl.BlockSpec((1, 2, block), lambda i: (0, 0, i)),
        ],
        out_shape=[
            jax.ShapeDtypeStruct((length, 128), BF16),
            jax.ShapeDtypeStruct((1, 2, length), F32),
        ],
        scratch_shapes=[pltpu.VMEM((128, length), BF16)],
        compiler_params=pltpu.CompilerParams(vmem_limit_bytes=44 << 20),
        cost_estimate=pl.CostEstimate(
            flops=32 * length * length * HD,
            transcendentals=2 * length * length,
            bytes_accessed=8 * length * 128,
        ),
        name="attend_forward",
    )(query, keys, values)


def backward_kernel(
    q_ref, k_ref, v_ref, c_ref, g_ref, total_ref, dq_ref, dk_ref, dv_ref, sum_ref, inner_ref
):
    step = pl.program_id(0)

    @pl.when(step == 0)
    def _():
        product = g_ref[...].astype(F32) * c_ref[...].astype(F32)
        upper = product.astype(BF16)
        lower = (product - upper.astype(F32)).astype(BF16)
        row = lax.broadcasted_iota(jnp.int32, (8, 128), 0)
        column = lax.broadcasted_iota(jnp.int32, (8, 128), 1)
        pick = jnp.where(
            (column >= HD * row) & (column < HD * row + HD), 1.0, 0.0
        ).astype(BF16)
        inner_ref[...] = lax.dot_general(
            pick, upper, NT, preferred_element_type=F32
        ) + lax.dot_general(pick, lower, NT, preferred_element_type=F32)

    keys = k_ref[...] * jnp.asarray(0.125, BF16)
    values = v_ref[...]
    flipped = jnp.transpose(keys)
    lane = lax.broadcasted_iota(jnp.int32, keys.shape, 1)
    nothing = jnp.zeros_like(keys)
    value_grads, key_grads, query_grads = [], [], []
    for head in range(2):
        own = (lane >= HD * head) & (lane < HD * head + HD)
        scores = lax.dot_general(
            jnp.where(own, keys, nothing), q_ref[...], NT, preferred_element_type=F32
        )
        probs = jnp.exp(scores - total_ref[0, head : head + 1, :])
        value_grads.append(
            lax.dot_general(probs.astype(BF16), g_ref[...], NN, preferred_element_type=F32)
        )
        prob_grad = lax.dot_general(
            jnp.where(own, values, nothing), g_ref[...], NT, preferred_element_type=F32
        )
        score_grad = (probs * (prob_grad - inner_ref[head : head + 1, :])).astype(BF16)
        key_grads.append(
            lax.dot_general(score_grad, q_ref[...], NN, preferred_element_type=F32)
        )
        query_grads.append(
            lax.dot_general(
                flipped[HD * head : HD * head + HD, :],
                score_grad,
                NN,
                preferred_element_type=F32,
            )
        )
    first = lane < HD
    dk_ref[...] = (jnp.where(first, key_grads[0], key_grads[1]) * 0.125).astype(BF16)
    dv_ref[...] = jnp.where(first, value_grads[0], value_grads[1]).astype(BF16)
    query_grad = jnp.concatenate(query_grads, axis=0)

    @pl.when(step == 0)
    def _():
        sum_ref[...] = query_grad

    @pl.when(step > 0)
    def _():
        sum_ref[...] += query_grad

    @pl.when(step == pl.num_programs(0) - 1)
    def _():
        dq_ref[...] = jnp.transpose(sum_ref[...]).astype(BF16)


def attend_backward(query, keys, values, context, grad, totals, pair, block):
    length = query.shape[0]
    whole = pl.BlockSpec((length, 128), lambda j: (0, pair))
    part = pl.BlockSpec((block, 128), lambda j: (j, pair))
    single = pl.BlockSpec((length, 128), lambda j: (0, 0))
    out_part = pl.BlockSpec((block, 128), lambda j: (j, 0))
    return pl.pallas_call(
        backward_kernel,
        grid=(length // block,),
        in_specs=[
            whole,
            part,
            part,
            single,
            whole,
            pl.BlockSpec((1, 2, length), lambda j: (0, 0, 0)),
        ],
        out_specs=[single, out_part, out_part],
        out_shape=[jax.ShapeDtypeStruct((length, 128), BF16)] * 3,
        scratch_shapes=[pltpu.VMEM((128, length), F32), pltpu.VMEM((8, length), F32)],
        compiler_params=pltpu.CompilerParams(vmem_limit_bytes=48 << 20),
        cost_estimate=pl.CostEstimate(
            flops=80 * length * length * HD,
            transcendentals=2 * length * length,
            bytes_accessed=20 * length * 128,
        ),
        name="attend_backward",
    )(query, keys, values, context, grad, totals)


def swap(value, axis, mask, size):
    return lax.ppermute(value, axis, [(i, i ^ mask) for i in range(size)])


def bits_of(axis, size):
    mine = lax.axis_index(axis)
    count = size.bit_length() - 1
    return [(axis, 1 << b, size, (mine >> b) & 1) for b in reversed(range(count))]


def split(value, bit, at):
    keep = lax.dynamic_index_in_dim(value, bit, at, keepdims=False)
    away = lax.dynamic_index_in_dim(value, 1 - bit, at, keepdims=False)
    return keep, away


def add(*values, dtype=BF16):
    total = values[0].astype(F32)
    for value in values[1:]:
        total = total + value.astype(F32)
    return total.astype(dtype)


def hold(value, *others):
    return lax.optimization_barrier((value,) + others)[0]


def in_number_order(pieces, mine):
    pieces = list(pieces)
    step = 1
    while step < len(pieces):
        flip = (mine & step) != 0
        for i in range(len(pieces)):
            if not i & step:
                a, b = pieces[i], pieces[i | step]
                pieces[i] = jnp.where(flip, b, a)
                pieces[i | step] = jnp.where(flip, a, b)
        step *= 2
    return pieces


def gather_blocks(value, axis, size, masks):
    held = {0: value}
    for mask in masks:
        held.update({r ^ mask: swap(piece, axis, mask, size) for r, piece in list(held.items())})
    return held


def gather_direct(value, axis, size, step=1):
    mine = lax.axis_index(axis) // step
    pieces = [value] + [swap(value, axis, r, size) for r in range(step, size, step)]
    return jnp.stack(in_number_order(pieces, mine))


def gather_core(value, size, at):
    other = swap(value, "shard", 1, size)
    bit = lax.axis_index("shard") & 1
    low = jnp.where(bit == 1, other, value)
    high = jnp.where(bit == 1, value, other)
    return jnp.stack([low, high], axis=at)


def scatter_direct(value, axis, size, step=1):
    mine = lax.axis_index(axis) // step
    parts = [lax.dynamic_index_in_dim(value, mine, 0, keepdims=False)]
    for r in range(1, size // step):
        away = lax.dynamic_index_in_dim(value, mine ^ r, 0, keepdims=False)
        parts.append(swap(away, axis, r * step, size))
    return parts


def body(
    seqs,
    shards,
    layer_input,
    cotangent,
    weight_qkv,
    weight_merge,
    weight_expand,
    weight_shrink,
    norm_gains,
    all_biases,
    bias_hidden,
    moment_qkv,
    moment_merge,
    moment_expand,
    moment_shrink,
    moment_gains,
    moment_biases,
    moment_hidden,
    squares_qkv,
    squares_merge,
    squares_expand,
    squares_shrink,
    squares_gains,
    squares_biases,
    squares_hidden,
):
    params = (
        weight_qkv,
        weight_merge,
        weight_expand,
        weight_shrink,
        norm_gains,
        all_biases,
        bias_hidden,
    )
    moments = (
        moment_qkv,
        moment_merge,
        moment_expand,
        moment_shrink,
        moment_gains,
        moment_biases,
        moment_hidden,
    )
    squares = (
        squares_qkv,
        squares_merge,
        squares_expand,
        squares_shrink,
        squares_gains,
        squares_biases,
        squares_hidden,
    )
    devices = seqs * shards
    far = shards // 2
    mine = lax.axis_index("seq")
    core = lax.axis_index("shard") & 1
    masks = [1 << b for b in range(seqs.bit_length() - 1)]
    tokens = layer_input[0]
    count, width = tokens.shape
    half = count // 2
    local = width // seqs
    pairs = local // 128
    hidden_width = bias_hidden.shape[0] * devices
    part = norm_gains.shape[1]

    by_heads = weight_qkv.astype(BF16).reshape(-1, 3, seqs, local)
    by_heads = by_heads.transpose(2, 0, 1, 3).reshape(seqs, -1, 3 * local)
    own_qkv = jnp.stack(in_number_order(scatter_direct(by_heads, "seq", seqs), mine))

    upper = gather_blocks(tokens[:half], "seq", seqs, masks)
    lower = gather_blocks(tokens[half:], "seq", seqs, masks[::-1])

    each = own_qkv.shape[0] * own_qkv.shape[1]
    own_bias = all_biases[1:3].astype(BF16).reshape(1, 2 * part)
    own_qkv = jnp.concatenate(
        [
            own_qkv.reshape(each, 3 * local),
            jnp.pad(own_bias, ((0, 7), (0, 3 * local - 2 * part))),
        ],
        axis=0,
    )
    own_qkv = gather_direct(own_qkv, "shard", shards, 2)
    own_qkv = gather_core(own_qkv, shards, 1)
    own_bias = own_qkv[:, :, each, : 2 * part].astype(F32).reshape(shards, 2, part)
    own_bias = own_bias.transpose(1, 0, 2).reshape(2, local)
    own_qkv = own_qkv[:, :, :each].reshape(far, 2, seqs, -1, 3 * local)
    own_qkv = own_qkv.transpose(2, 0, 1, 3, 4).reshape(width, 3 * local)

    deep = weight_expand.shape[0]
    small = jnp.concatenate(
        [
            norm_gains.astype(BF16).reshape(-1),
            all_biases.astype(BF16).reshape(-1),
            bias_hidden.astype(BF16),
        ]
    ).reshape(deep, -1)
    thin = small.shape[1]
    mixed = jnp.concatenate(
        [
            weight_expand.astype(BF16),
            weight_merge.astype(BF16),
            jnp.pad(small, ((0, 0), (0, 128 - thin))),
        ],
        axis=1,
    )
    mixed = lax.all_gather(mixed, ("seq", "shard"), axis=0, tiled=True)
    full_expand = mixed[:, :hidden_width]
    full_merge = mixed[:, hidden_width : hidden_width + width]
    full_shrink = lax.all_gather(weight_shrink.astype(BF16), ("seq", "shard"), axis=0, tiled=True)
    small = mixed[:, hidden_width + width : hidden_width + width + thin].reshape(devices, -1).astype(F32)
    rows = small[:, : 8 * part].reshape(devices, 8, part).transpose(1, 0, 2).reshape(8, width)
    gains, biases = rows[:2], rows[2:]
    hidden_bias = small[:, 8 * part :].reshape(hidden_width)

    every = jnp.concatenate(
        [piece for r in range(seqs) for piece in (upper[r], lower[r])], axis=0
    )

    bias_row = jnp.concatenate([own_bias[0], jnp.zeros((local,), F32), own_bias[1]])
    qkv = (jnp.dot(every, own_qkv, preferred_element_type=F32) + bias_row).astype(BF16)
    query, keys, values = qkv[:, :local], qkv[:, local : 2 * local], qkv[:, 2 * local :]
    length = qkv.shape[0]
    block = min(512, length)
    contexts, totals, arrived = [], [], []
    for pair in range(pairs):
        context_pair, total = attend_forward(query, keys, values, pair, block)
        contexts.append(context_pair)
        totals.append(total)
        arrived.append(
            in_number_order(
                [
                    swap(context_pair[r * count : (r + 1) * count], "seq", r, seqs)
                    if r
                    else context_pair[:count]
                    for r in range(seqs)
                ],
                mine,
            )
        )
    context = jnp.concatenate(
        [arrived[pair][s] for s in range(seqs) for pair in range(pairs)], axis=1
    )

    attended = jnp.dot(context, full_merge, preferred_element_type=F32) + biases[3]
    first, normed_one, inverse_one = norm_forward(
        tokens.astype(F32) + attended, gains[0], biases[0]
    )
    first_low = first.astype(BF16)
    hidden = jnp.dot(first_low, full_expand, preferred_element_type=F32) + hidden_bias
    active = (hidden * normal_share(hidden)).astype(BF16)
    branch = jnp.dot(active, full_shrink, preferred_element_type=F32) + biases[5]
    result, normed_two, inverse_two = norm_forward(first + branch, gains[1], biases[4])
    grad_out = cotangent[0]
    grad_gain_two = jnp.sum(grad_out * normed_two, axis=0)
    grad_shift_two = jnp.sum(grad_out, axis=0)
    grad_mid = norm_backward(grad_out, normed_two, inverse_two, gains[1])
    grad_branch = grad_mid.astype(BF16)
    grad_shrink_bias = jnp.sum(grad_branch, axis=0, dtype=F32)

    def core_step(left, right, extra=None):
        grad = lax.dot_general(left, right, TN, preferred_element_type=F32).astype(BF16)
        grad = grad.reshape(seqs, far, 2, -1, grad.shape[1])
        if extra is not None:
            grad = jnp.concatenate([grad, extra], axis=-1)
        keep, away = split(grad, core, 2)
        return keep, swap(away, "shard", 1, shards), away

    def halving_start(grad, way):
        grad = grad.reshape((2,) * len(masks) + grad.shape[1:])
        return halving_send(grad, masks[::-1], way)

    def halving_send(grad, left, way):
        mask = way[0]
        keep, away = split(grad, (mine // mask) & 1, left.index(mask))
        left = [m for m in left if m != mask]
        return keep, swap(away, "seq", mask, seqs), away, left, way[1:]

    def halving_next(started, *others):
        if not isinstance(started, tuple):
            return started
        keep, got, _, left, way = started
        grad = add(keep, hold(got, *others))
        return halving_send(grad, left, way) if way else grad

    grad_shrink = lax.dot_general(active, grad_branch, TN, preferred_element_type=F32).astype(BF16)
    summed_shrink = lax.psum_scatter(
        grad_shrink, ("seq", "shard"), scatter_dimension=0, tiled=True
    ).astype(F32)
    grad_branch = hold(grad_branch, grad_shrink)
    grad_active = lax.dot_general(grad_branch, full_shrink, NT, preferred_element_type=F32)
    grad_hidden = (grad_active * gelu_slope(hidden)).astype(BF16)
    grad_hidden_bias = jnp.sum(grad_hidden, axis=0, dtype=F32)
    grad_first = grad_mid + lax.dot_general(
        grad_hidden, full_expand, NT, preferred_element_type=F32
    )
    grad_gain_one = jnp.sum(grad_first * normed_one, axis=0)
    grad_shift_one = jnp.sum(grad_first, axis=0)
    grad_residual = norm_backward(grad_first, normed_one, inverse_one, gains[0])
    grad_attended = grad_residual.astype(BF16)
    grad_merge_bias = jnp.sum(grad_attended, axis=0, dtype=F32)
    grad_heads = lax.dot_general(
        grad_attended, full_merge, NT, preferred_element_type=F32
    ).astype(BF16)
    grad_heads = grad_heads.reshape(count, seqs, local).transpose(1, 0, 2)
    grad_context = jnp.concatenate(scatter_direct(grad_heads, "seq", seqs), axis=0)
    small_grads = jnp.concatenate(
        [
            jnp.stack(
                [
                    grad_gain_one,
                    grad_gain_two,
                    grad_shift_one,
                    grad_merge_bias,
                    grad_shift_two,
                    grad_shrink_bias,
                ]
            )
            .reshape(6, devices, part)
            .transpose(1, 0, 2)
            .reshape(devices, 6 * part),
            grad_hidden_bias.reshape(devices, -1),
        ],
        axis=1,
    )
    small_grads = small_grads.astype(BF16).reshape(seqs, far, 2, deep, -1)
    slim = small_grads.shape[-1]
    small_grads = jnp.pad(small_grads, ((0, 0),) * 4 + ((0, 128 - slim),))
    merge_keep, merge_got, merge_away = core_step(context, grad_attended, small_grads)
    expand_keep, expand_got, expand_away = core_step(hold(first_low, grad_heads), grad_hidden)
    grad_context = hold(grad_context, merge_away, expand_away)

    grads = []
    for pair in range(pairs):
        grads.append(
            attend_backward(
                query, keys, values, contexts[pair], grad_context, totals[pair], pair, block
            )
        )
        if pair == 0:
            merge = halving_start(add(merge_keep, hold(merge_got, grads[0][0])), masks)
            expand = add(expand_keep, hold(expand_got, grads[0][0]))
            middle = expand.shape[-1] // 2
            expand = [
                halving_start(expand[..., :middle], masks),
                halving_start(expand[..., middle:], masks[::-1]),
            ]
            grad_context = hold(grad_context, merge[2], *[part[2] for part in expand])
    grad_rows = jnp.concatenate(
        [grads[pair][which] for which in range(3) for pair in range(pairs)], axis=1
    )

    spread = lax.dot_general(grad_rows, own_qkv, NT, preferred_element_type=F32).astype(BF16)
    spread = lax.optimization_barrier(spread)
    spread = spread.reshape(seqs, count, width)
    spread = [spread[0]] + [swap(spread[r], "seq", r, seqs) for r in reversed(range(1, seqs))]

    head_sums = jnp.stack(
        [
            jnp.sum(grad_rows[:, :local], axis=0, dtype=F32).reshape(shards, part),
            jnp.sum(grad_rows[:, 2 * local :], axis=0, dtype=F32).reshape(shards, part),
        ],
        axis=1,
    )
    head_sums = head_sums.astype(BF16).reshape(1, far, 2, deep, 2)
    head_sums = jnp.broadcast_to(
        jnp.pad(head_sums, ((0, 0),) * 4 + ((0, 126),)), (seqs, far, 2, deep, 128)
    )
    keep, got, away = core_step(every, grad_rows, head_sums)

    while isinstance(merge, tuple):
        merge = halving_next(merge, grad_rows)
        expand = [halving_next(part, grad_rows) for part in expand]
    others = scatter_direct(jnp.concatenate(expand + [merge], axis=-1), "shard", shards, 2)
    grad_weight = add(keep, got).transpose(1, 0, 2, 3)
    grad_weight = scatter_direct(grad_weight, "shard", shards, 2)
    spread = spread[:1] + [hold(piece, grad_weight[0], others[0]) for piece in spread[1:]]
    grad_input = add(grad_residual, *spread, dtype=F32)
    arrived = scatter_direct(add(*grad_weight), "seq", seqs)
    head_sums = arrived[0][:, 3 * local : 3 * local + 2].astype(F32).reshape(2, part)
    summed_qkv = in_number_order([piece[:, : 3 * local] for piece in arrived], mine)
    summed_qkv = (
        jnp.stack([piece.reshape(-1, 3, local) for piece in summed_qkv], axis=2)
        .reshape(-1, 3 * width)
        .astype(F32)
    )
    others = add(*others, dtype=F32)
    summed_expand = others[:, :hidden_width]
    summed_merge = others[:, hidden_width : hidden_width + width]
    small_grads = others[:, hidden_width + width :][:, :slim].reshape(-1)

    small_rows = small_grads[: 6 * part].reshape(6, part)
    summed = (
        summed_qkv,
        summed_merge,
        summed_expand,
        summed_shrink,
        small_rows[:2],
        jnp.concatenate([small_rows[2:3], head_sums, small_rows[3:]], axis=0),
        small_grads[6 * part :],
    )
    finals = []
    momenta = []
    squared_all = []
    for index in range(7):
        master, change, momentum, squared = adam_update(
            params[index], summed[index], moments[index], squares[index], index < 4
        )
        finals.append(master if index < 4 else change)
        momenta.append(momentum)
        squared_all.append(squared)
    layer_output = result.astype(BF16)[None]
    return (
        (layer_output, grad_input[None])
        + summed
        + tuple(finals)
        + tuple(momenta)
        + tuple(squared_all)
    )


def solution(mesh):
    both = ("seq", "shard")
    rows, columns, flat = P(both, None), P(None, both), P(both)
    group = (rows, rows, rows, rows, columns, columns, flat)
    states = P("shard", "seq", None)
    return jax.shard_map(
        functools.partial(body, mesh.shape["seq"], mesh.shape["shard"]),
        mesh=mesh,
        in_specs=(states, states) + group * 3,
        out_specs=(states, states) + group * 4,
        check_vma=False,
    )
```

```python
import functools

import jax
import jax.numpy as jnp
from jax import lax
from jax.experimental import pallas as pl
from jax.experimental.pallas import tpu as pltpu
from jax.sharding import PartitionSpec as P

HD = 64
STEP = 10
F32 = jnp.float32
BF16 = jnp.bfloat16
NT = (((1,), (1,)), ((), ()))
NN = (((1,), (0,)), ((), ()))
TN = (((0,), (0,)), ((), ()))


def norm_forward(value, gain, shift):
    centre = value - jnp.mean(value, axis=-1, keepdims=True)
    inverse = lax.rsqrt(jnp.mean(centre * centre, axis=-1, keepdims=True) + 1e-06)
    normed = centre * inverse
    return (normed * gain + shift, normed, inverse)


def norm_backward(grad, normed, inverse, gain):
    scaled = grad * gain
    inner = jnp.mean(scaled * normed, axis=-1, keepdims=True)
    return inverse * (scaled - jnp.mean(scaled, axis=-1, keepdims=True) - normed * inner)


def normal_share(hidden):
    return 0.5 * (1.0 + lax.erf(hidden * 0.7071067811865476))


def gelu_slope(hidden):
    return normal_share(hidden) + hidden * jnp.exp(-0.5 * hidden * hidden) * 0.3989422804014327


def adam_update(param, grad, moment, squares, decay):
    momentum = 0.9 * moment + 0.1 * grad
    squared = 0.999 * squares + 0.001 * grad * grad
    update = momentum / (1.0 - 0.9**STEP) / (jnp.sqrt(squared / (1.0 - 0.999**STEP)) + 1e-08)
    if decay:
        update = update + 0.01 * param
    change = -0.02 * update
    return (param - 0.02 * update, change, momentum, squared)


def forward_kernel(q_ref, k_ref, v_ref, c_ref, total_ref, flipped_ref):
    @pl.when(pl.program_id(0) == 0)
    def _():
        flipped_ref[...] = jnp.transpose(v_ref[...])

    query = q_ref[...] * jnp.asarray(0.125, BF16)
    lane = lax.broadcasted_iota(jnp.int32, query.shape, 1)
    pieces, rows = [], []
    for head in range(2):
        own = (lane >= HD * head) & (lane < HD * head + HD)
        scores = lax.dot_general(
            k_ref[...], jnp.where(own, query, jnp.zeros_like(query)), NT, preferred_element_type=F32
        )
        highest = jnp.max(scores, axis=0, keepdims=True)
        weights = jnp.exp(scores - highest)
        total = jnp.sum(weights, axis=0, keepdims=True)
        context = lax.dot_general(
            flipped_ref[HD * head : HD * head + HD, :],
            weights.astype(BF16),
            NN,
            preferred_element_type=F32,
        )
        pieces.append(context * (1.0 / total))
        rows.append(highest + jnp.log(total))
    c_ref[...] = jnp.transpose(jnp.concatenate(pieces, axis=0)).astype(BF16)
    total_ref[...] = jnp.concatenate(rows, axis=0)[None]


def attend_forward(query, keys, values, pair, block):
    length = query.shape[0]
    whole = pl.BlockSpec((length, 128), lambda i: (0, pair))
    return pl.pallas_call(
        forward_kernel,
        grid=(length // block,),
        in_specs=[pl.BlockSpec((block, 128), lambda i: (i, pair)), whole, whole],
        out_specs=[
            pl.BlockSpec((block, 128), lambda i: (i, 0)),
            pl.BlockSpec((1, 2, block), lambda i: (0, 0, i)),
        ],
        out_shape=[
            jax.ShapeDtypeStruct((length, 128), BF16),
            jax.ShapeDtypeStruct((1, 2, length), F32),
        ],
        scratch_shapes=[pltpu.VMEM((128, length), BF16)],
        compiler_params=pltpu.CompilerParams(vmem_limit_bytes=44 << 20),
        cost_estimate=pl.CostEstimate(
            flops=32 * length * length * HD,
            transcendentals=2 * length * length,
            bytes_accessed=8 * length * 128,
        ),
        name="attend_forward",
    )(query, keys, values)


def backward_kernel(
    q_ref, k_ref, v_ref, c_ref, g_ref, total_ref, dq_ref, dk_ref, dv_ref, sum_ref, inner_ref
):
    step = pl.program_id(0)

    @pl.when(step == 0)
    def _():
        product = g_ref[...].astype(F32) * c_ref[...].astype(F32)
        upper = product.astype(BF16)
        lower = (product - upper.astype(F32)).astype(BF16)
        row = lax.broadcasted_iota(jnp.int32, (8, 128), 0)
        column = lax.broadcasted_iota(jnp.int32, (8, 128), 1)
        pick = jnp.where(
            (column >= HD * row) & (column < HD * row + HD), 1.0, 0.0
        ).astype(BF16)
        inner_ref[...] = lax.dot_general(
            pick, upper, NT, preferred_element_type=F32
        ) + lax.dot_general(pick, lower, NT, preferred_element_type=F32)

    keys = k_ref[...] * jnp.asarray(0.125, BF16)
    values = v_ref[...]
    flipped = jnp.transpose(keys)
    lane = lax.broadcasted_iota(jnp.int32, keys.shape, 1)
    nothing = jnp.zeros_like(keys)
    value_grads, key_grads, query_grads = [], [], []
    for head in range(2):
        own = (lane >= HD * head) & (lane < HD * head + HD)
        scores = lax.dot_general(
            jnp.where(own, keys, nothing), q_ref[...], NT, preferred_element_type=F32
        )
        probs = jnp.exp(scores - total_ref[0, head : head + 1, :])
        value_grads.append(
            lax.dot_general(probs.astype(BF16), g_ref[...], NN, preferred_element_type=F32)
        )
        prob_grad = lax.dot_general(
            jnp.where(own, values, nothing), g_ref[...], NT, preferred_element_type=F32
        )
        score_grad = (probs * (prob_grad - inner_ref[head : head + 1, :])).astype(BF16)
        key_grads.append(
            lax.dot_general(score_grad, q_ref[...], NN, preferred_element_type=F32)
        )
        query_grads.append(
            lax.dot_general(
                flipped[HD * head : HD * head + HD, :],
                score_grad,
                NN,
                preferred_element_type=F32,
            )
        )
    first = lane < HD
    dk_ref[...] = (jnp.where(first, key_grads[0], key_grads[1]) * 0.125).astype(BF16)
    dv_ref[...] = jnp.where(first, value_grads[0], value_grads[1]).astype(BF16)
    query_grad = jnp.concatenate(query_grads, axis=0)

    @pl.when(step == 0)
    def _():
        sum_ref[...] = query_grad

    @pl.when(step > 0)
    def _():
        sum_ref[...] += query_grad

    @pl.when(step == pl.num_programs(0) - 1)
    def _():
        dq_ref[...] = jnp.transpose(sum_ref[...]).astype(BF16)


def attend_backward(query, keys, values, context, grad, totals, pair, block):
    length = query.shape[0]
    whole = pl.BlockSpec((length, 128), lambda j: (0, pair))
    part = pl.BlockSpec((block, 128), lambda j: (j, pair))
    single = pl.BlockSpec((length, 128), lambda j: (0, 0))
    out_part = pl.BlockSpec((block, 128), lambda j: (j, 0))
    return pl.pallas_call(
        backward_kernel,
        grid=(length // block,),
        in_specs=[
            whole,
            part,
            part,
            single,
            whole,
            pl.BlockSpec((1, 2, length), lambda j: (0, 0, 0)),
        ],
        out_specs=[single, out_part, out_part],
        out_shape=[jax.ShapeDtypeStruct((length, 128), BF16)] * 3,
        scratch_shapes=[pltpu.VMEM((128, length), F32), pltpu.VMEM((8, length), F32)],
        compiler_params=pltpu.CompilerParams(vmem_limit_bytes=48 << 20),
        cost_estimate=pl.CostEstimate(
            flops=80 * length * length * HD,
            transcendentals=2 * length * length,
            bytes_accessed=20 * length * 128,
        ),
        name="attend_backward",
    )(query, keys, values, context, grad, totals)


def swap(value, axis, mask, size):
    return lax.ppermute(value, axis, [(i, i ^ mask) for i in range(size)])


def bits_of(axis, size):
    mine = lax.axis_index(axis)
    count = size.bit_length() - 1
    return [(axis, 1 << b, size, (mine >> b) & 1) for b in reversed(range(count))]


def split(value, bit, at):
    keep = lax.dynamic_index_in_dim(value, bit, at, keepdims=False)
    away = lax.dynamic_index_in_dim(value, 1 - bit, at, keepdims=False)
    return keep, away


def add(*values, dtype=BF16):
    total = values[0].astype(F32)
    for value in values[1:]:
        total = total + value.astype(F32)
    return total.astype(dtype)


def hold(value, *others):
    return lax.optimization_barrier((value,) + others)[0]


def in_number_order(pieces, mine):
    pieces = list(pieces)
    step = 1
    while step < len(pieces):
        flip = (mine & step) != 0
        for i in range(len(pieces)):
            if not i & step:
                a, b = pieces[i], pieces[i | step]
                pieces[i] = jnp.where(flip, b, a)
                pieces[i | step] = jnp.where(flip, a, b)
        step *= 2
    return pieces


def gather_blocks(value, axis, size, masks):
    held = {0: value}
    for mask in masks:
        held.update({r ^ mask: swap(piece, axis, mask, size) for r, piece in list(held.items())})
    return held


def gather_direct(value, axis, size, step=1):
    mine = lax.axis_index(axis) // step
    pieces = [value] + [swap(value, axis, r, size) for r in range(step, size, step)]
    return jnp.stack(in_number_order(pieces, mine))


def gather_core(value, size, at):
    other = swap(value, "shard", 1, size)
    bit = lax.axis_index("shard") & 1
    low = jnp.where(bit == 1, other, value)
    high = jnp.where(bit == 1, value, other)
    return jnp.stack([low, high], axis=at)


def scatter_direct(value, axis, size, step=1):
    mine = lax.axis_index(axis) // step
    parts = [lax.dynamic_index_in_dim(value, mine, 0, keepdims=False)]
    for r in range(1, size // step):
        away = lax.dynamic_index_in_dim(value, mine ^ r, 0, keepdims=False)
        parts.append(swap(away, axis, r * step, size))
    return parts


def body(
    seqs,
    shards,
    layer_input,
    cotangent,
    weight_qkv,
    weight_merge,
    weight_expand,
    weight_shrink,
    norm_gains,
    all_biases,
    bias_hidden,
    moment_qkv,
    moment_merge,
    moment_expand,
    moment_shrink,
    moment_gains,
    moment_biases,
    moment_hidden,
    squares_qkv,
    squares_merge,
    squares_expand,
    squares_shrink,
    squares_gains,
    squares_biases,
    squares_hidden,
):
    params = (
        weight_qkv,
        weight_merge,
        weight_expand,
        weight_shrink,
        norm_gains,
        all_biases,
        bias_hidden,
    )
    moments = (
        moment_qkv,
        moment_merge,
        moment_expand,
        moment_shrink,
        moment_gains,
        moment_biases,
        moment_hidden,
    )
    squares = (
        squares_qkv,
        squares_merge,
        squares_expand,
        squares_shrink,
        squares_gains,
        squares_biases,
        squares_hidden,
    )
    devices = seqs * shards
    far = shards // 2
    mine = lax.axis_index("seq")
    core = lax.axis_index("shard") & 1
    masks = [1 << b for b in range(seqs.bit_length() - 1)]
    tokens = layer_input[0]
    count, width = tokens.shape
    half = count // 2
    local = width // seqs
    pairs = local // 128
    hidden_width = bias_hidden.shape[0] * devices
    part = norm_gains.shape[1]

    by_heads = weight_qkv.astype(BF16).reshape(-1, 3, seqs, local)
    by_heads = by_heads.transpose(2, 0, 1, 3).reshape(seqs, -1, 3 * local)
    own_qkv = jnp.stack(in_number_order(scatter_direct(by_heads, "seq", seqs), mine))

    upper = gather_blocks(tokens[:half], "seq", seqs, masks)
    lower = gather_blocks(tokens[half:], "seq", seqs, masks[::-1])

    each = own_qkv.shape[0] * own_qkv.shape[1]
    own_bias = all_biases[1:3].astype(BF16).reshape(1, 2 * part)
    own_qkv = jnp.concatenate(
        [
            own_qkv.reshape(each, 3 * local),
            jnp.pad(own_bias, ((0, 7), (0, 3 * local - 2 * part))),
        ],
        axis=0,
    )
    own_qkv = gather_direct(own_qkv, "shard", shards, 2)
    own_qkv = gather_core(own_qkv, shards, 1)
    own_bias = own_qkv[:, :, each, : 2 * part].astype(F32).reshape(shards, 2, part)
    own_bias = own_bias.transpose(1, 0, 2).reshape(2, local)
    own_qkv = own_qkv[:, :, :each].reshape(far, 2, seqs, -1, 3 * local)
    own_qkv = own_qkv.transpose(2, 0, 1, 3, 4).reshape(width, 3 * local)

    deep = weight_expand.shape[0]
    small = jnp.concatenate(
        [
            norm_gains.astype(BF16).reshape(-1),
            all_biases.astype(BF16).reshape(-1),
            bias_hidden.astype(BF16),
        ]
    ).reshape(deep, -1)
    thin = small.shape[1]
    mixed = jnp.concatenate(
        [
            weight_expand.astype(BF16),
            weight_merge.astype(BF16),
            jnp.pad(small, ((0, 0), (0, 128 - thin))),
        ],
        axis=1,
    )
    mixed = lax.all_gather(mixed, ("seq", "shard"), axis=0, tiled=True)
    full_expand = mixed[:, :hidden_width]
    full_merge = mixed[:, hidden_width : hidden_width + width]
    full_shrink = lax.all_gather(weight_shrink.astype(BF16), ("seq", "shard"), axis=0, tiled=True)
    small = mixed[:, hidden_width + width : hidden_width + width + thin].reshape(devices, -1).astype(F32)
    rows = small[:, : 8 * part].reshape(devices, 8, part).transpose(1, 0, 2).reshape(8, width)
    gains, biases = rows[:2], rows[2:]
    hidden_bias = small[:, 8 * part :].reshape(hidden_width)

    every = jnp.concatenate(
        [piece for r in range(seqs) for piece in (upper[r], lower[r])], axis=0
    )

    bias_row = jnp.concatenate([own_bias[0], jnp.zeros((local,), F32), own_bias[1]])
    qkv = (jnp.dot(every, own_qkv, preferred_element_type=F32) + bias_row).astype(BF16)
    query, keys, values = qkv[:, :local], qkv[:, local : 2 * local], qkv[:, 2 * local :]
    length = qkv.shape[0]
    block = min(512, length)
    contexts, totals, arrived = [], [], []
    for pair in range(pairs):
        context_pair, total = attend_forward(query, keys, values, pair, block)
        contexts.append(context_pair)
        totals.append(total)
        arrived.append(
            in_number_order(
                [
                    swap(context_pair[r * count : (r + 1) * count], "seq", r, seqs)
                    if r
                    else context_pair[:count]
                    for r in range(seqs)
                ],
                mine,
            )
        )
    context = jnp.concatenate(
        [arrived[pair][s] for s in range(seqs) for pair in range(pairs)], axis=1
    )

    attended = jnp.dot(context, full_merge, preferred_element_type=F32) + biases[3]
    first, normed_one, inverse_one = norm_forward(
        tokens.astype(F32) + attended, gains[0], biases[0]
    )
    first_low = first.astype(BF16)
    hidden = jnp.dot(first_low, full_expand, preferred_element_type=F32) + hidden_bias
    active = (hidden * normal_share(hidden)).astype(BF16)
    branch = jnp.dot(active, full_shrink, preferred_element_type=F32) + biases[5]
    result, normed_two, inverse_two = norm_forward(first + branch, gains[1], biases[4])
    grad_out = cotangent[0]
    grad_gain_two = jnp.sum(grad_out * normed_two, axis=0)
    grad_shift_two = jnp.sum(grad_out, axis=0)
    grad_mid = norm_backward(grad_out, normed_two, inverse_two, gains[1])
    grad_branch = grad_mid.astype(BF16)
    grad_shrink_bias = jnp.sum(grad_branch, axis=0, dtype=F32)

    def core_step(left, right, extra=None):
        grad = lax.dot_general(left, right, TN, preferred_element_type=F32).astype(BF16)
        grad = grad.reshape(seqs, far, 2, -1, grad.shape[1])
        if extra is not None:
            grad = jnp.concatenate([grad, extra], axis=-1)
        keep, away = split(grad, core, 2)
        return keep, swap(away, "shard", 1, shards), away

    def halving_start(grad, way):
        grad = grad.reshape((2,) * len(masks) + grad.shape[1:])
        return halving_send(grad, masks[::-1], way)

    def halving_send(grad, left, way):
        mask = way[0]
        keep, away = split(grad, (mine // mask) & 1, left.index(mask))
        left = [m for m in left if m != mask]
        return keep, swap(away, "seq", mask, seqs), away, left, way[1:]

    def halving_next(started, *others):
        if not isinstance(started, tuple):
            return started
        keep, got, _, left, way = started
        grad = add(keep, hold(got, *others))
        return halving_send(grad, left, way) if way else grad

    grad_shrink = lax.dot_general(active, grad_branch, TN, preferred_element_type=F32).astype(BF16)
    summed_shrink = lax.psum_scatter(
        grad_shrink, ("seq", "shard"), scatter_dimension=0, tiled=True
    ).astype(F32)
    grad_branch = hold(grad_branch, grad_shrink)
    grad_active = lax.dot_general(grad_branch, full_shrink, NT, preferred_element_type=F32)
    grad_hidden = (grad_active * gelu_slope(hidden)).astype(BF16)
    grad_hidden_bias = jnp.sum(grad_hidden, axis=0, dtype=F32)
    grad_first = grad_mid + lax.dot_general(
        grad_hidden, full_expand, NT, preferred_element_type=F32
    )
    grad_gain_one = jnp.sum(grad_first * normed_one, axis=0)
    grad_shift_one = jnp.sum(grad_first, axis=0)
    grad_residual = norm_backward(grad_first, normed_one, inverse_one, gains[0])
    grad_attended = grad_residual.astype(BF16)
    grad_merge_bias = jnp.sum(grad_attended, axis=0, dtype=F32)
    grad_heads = lax.dot_general(
        grad_attended, full_merge, NT, preferred_element_type=F32
    ).astype(BF16)
    grad_heads = grad_heads.reshape(count, seqs, local).transpose(1, 0, 2)
    grad_context = jnp.concatenate(scatter_direct(grad_heads, "seq", seqs), axis=0)
    small_grads = jnp.concatenate(
        [
            jnp.stack(
                [
                    grad_gain_one,
                    grad_gain_two,
                    grad_shift_one,
                    grad_merge_bias,
                    grad_shift_two,
                    grad_shrink_bias,
                ]
            )
            .reshape(6, devices, part)
            .transpose(1, 0, 2)
            .reshape(devices, 6 * part),
            grad_hidden_bias.reshape(devices, -1),
        ],
        axis=1,
    )
    small_grads = small_grads.astype(BF16).reshape(seqs, far, 2, deep, -1)
    slim = small_grads.shape[-1]
    small_grads = jnp.pad(small_grads, ((0, 0),) * 4 + ((0, 128 - slim),))
    merge_keep, merge_got, merge_away = core_step(context, grad_attended, small_grads)
    expand_keep, expand_got, expand_away = core_step(hold(first_low, grad_heads), grad_hidden)
    grad_context = hold(grad_context, merge_away, expand_away)

    grads = []
    for pair in range(pairs):
        grads.append(
            attend_backward(
                query, keys, values, contexts[pair], grad_context, totals[pair], pair, block
            )
        )
        if pair == 0:
            merge = halving_start(add(merge_keep, hold(merge_got, grads[0][0])), masks)
            expand = add(expand_keep, hold(expand_got, grads[0][0]))
            middle = expand.shape[-1] // 2
            expand = [
                halving_start(expand[..., :middle], masks),
                halving_start(expand[..., middle:], masks[::-1]),
            ]
            grad_context = hold(grad_context, merge[2], *[part[2] for part in expand])
    grad_rows = jnp.concatenate(
        [grads[pair][which] for which in range(3) for pair in range(pairs)], axis=1
    )

    spread = lax.dot_general(grad_rows, own_qkv, NT, preferred_element_type=F32).astype(BF16)
    spread, grad_rows = lax.optimization_barrier((spread, grad_rows))
    spread = spread.reshape((2,) * len(masks) + (2, half, width))

    def spread_send(held, left, way):
        at = left.index(way[0])
        keep = lax.index_in_dim(held, 0, at, keepdims=False)
        away = lax.index_in_dim(held, 1, at, keepdims=False)
        left = [m for m in left if m != way[0]]
        return keep, swap(away, "seq", way[0], seqs), left, way[1:]

    sides = [
        spread_send(
            lax.index_in_dim(spread, side, len(masks), keepdims=False), masks[::-1], way
        )
        for side, way in ((0, masks), (1, masks[::-1]))
    ]

    head_sums = jnp.stack(
        [
            jnp.sum(grad_rows[:, :local], axis=0, dtype=F32).reshape(shards, part),
            jnp.sum(grad_rows[:, 2 * local :], axis=0, dtype=F32).reshape(shards, part),
        ],
        axis=1,
    )
    head_sums = head_sums.astype(BF16).reshape(1, far, 2, deep, 2)
    head_sums = jnp.broadcast_to(
        jnp.pad(head_sums, ((0, 0),) * 4 + ((0, 126),)), (seqs, far, 2, deep, 128)
    )
    keep, got, away = core_step(every, grad_rows, head_sums)

    while isinstance(merge, tuple):
        merge = halving_next(merge, grad_rows)
        expand = [halving_next(part, grad_rows) for part in expand]
        fence = [part[2] for part in expand if isinstance(part, tuple)]
        if sides[0][3]:
            sides = [
                spread_send(add(held, hold(arrived, *fence)), left, way)
                for held, arrived, left, way in sides
            ]
    while sides[0][3]:
        sides = [
            spread_send(add(held, arrived), left, way) for held, arrived, left, way in sides
        ]
    expand = [hold(part, sides[0][0], sides[1][0]) for part in expand]
    others = scatter_direct(jnp.concatenate(expand + [merge], axis=-1), "shard", shards, 2)
    grad_weight = add(keep, got).transpose(1, 0, 2, 3)
    grad_weight = scatter_direct(grad_weight, "shard", shards, 2)
    sides = [
        add(held, hold(arrived, grad_weight[0], others[0]), dtype=F32)
        for held, arrived, _, _ in sides
    ]
    grad_input = grad_residual + jnp.concatenate(sides, axis=0)
    arrived = scatter_direct(add(*grad_weight), "seq", seqs)
    arrived = arrived[:1] + [hold(piece, others[0]) for piece in arrived[1:]]
    head_sums = arrived[0][:, 3 * local : 3 * local + 2].astype(F32).reshape(2, part)
    summed_qkv = in_number_order([piece[:, : 3 * local] for piece in arrived], mine)
    summed_qkv = (
        jnp.stack([piece.reshape(-1, 3, local) for piece in summed_qkv], axis=2)
        .reshape(-1, 3 * width)
        .astype(F32)
    )
    others = add(*others, dtype=F32)
    summed_expand = others[:, :hidden_width]
    summed_merge = others[:, hidden_width : hidden_width + width]
    small_grads = others[:, hidden_width + width :][:, :slim].reshape(-1)

    small_rows = small_grads[: 6 * part].reshape(6, part)
    summed = (
        summed_qkv,
        summed_merge,
        summed_expand,
        summed_shrink,
        small_rows[:2],
        jnp.concatenate([small_rows[2:3], head_sums, small_rows[3:]], axis=0),
        small_grads[6 * part :],
    )
    finals = []
    momenta = []
    squared_all = []
    for index in range(7):
        master, change, momentum, squared = adam_update(
            params[index], summed[index], moments[index], squares[index], index < 4
        )
        finals.append(master if index < 4 else change)
        momenta.append(momentum)
        squared_all.append(squared)
    layer_output = result.astype(BF16)[None]
    return (
        (layer_output, grad_input[None])
        + summed
        + tuple(finals)
        + tuple(momenta)
        + tuple(squared_all)
    )


def solution(mesh):
    both = ("seq", "shard")
    rows, columns, flat = P(both, None), P(None, both), P(both)
    group = (rows, rows, rows, rows, columns, columns, flat)
    states = P("shard", "seq", None)
    return jax.shard_map(
        functools.partial(body, mesh.shape["seq"], mesh.shape["shard"]),
        mesh=mesh,
        in_specs=(states, states) + group * 3,
        out_specs=(states, states) + group * 4,
        check_vma=False,
    )
```
